32 devices in a mesh: fibre: 2 (over y), chan: 4 (over z), tm: 2 (over x), win: 2 (over core).
Axes of the slice: x: 2, y: 2, z: 4, core: 2. Of those that a mesh axis runs over, the one named last changes fastest.
Arguments:
- records: bfloat16 [64, 16, 16384], P(('fibre', 'chan'), 'win', 'tm'), parts along dimension 0, may hold values from -32 to 32, as said below
- filter_taps: bfloat16 [64], replicated, may hold values from -0.75 to 0.75
- segment_end: int32 [32], P(('fibre', 'win')), parts along dimension 0, may hold values from 8192 to 16384, as said below
- pair_mask: int32 [8, 3], P(('fibre', 'chan')), parts along dimension 0, may hold values 0 or 1
Outputs:
- correlation: float32 [3, 8, 64, 3840], P(None, 'win', ('fibre', 'chan', 'tm')), parts along dimension 2
The draws below stay inside these ranges and needn't reach their ends.
There are 2 independent parts, one for each index of `fibre`. The reference program is written for one: setup_inputs(seed, part) draws one part's arguments, and reference() takes and returns one part's arrays. A program takes and returns all parts, laid end to end along the dimension named above; an argument that names none is the same for every part. Nothing has to cross between parts.
Inputs may be any that keep to these rules, and one draw needn't show every extreme that they name: `records`: samples are clipped at the recorder's full scale. `segment_end`: samples of a window at or after this index are missing; some window is complete and some keeps only its first half.
All inputs are finite; a program needn't handle non-finite values. No bound on the sum of `pair_mask` on one device may be relied on, other than what follows from the above.
Results may differ from the reference program's by a relative error of at most 0.0047.
Values may be sent and summed in bfloat16 or wider, within the bound.
No kernel may reach another device: no remote copies, remote signals or barrier semaphores. Data moves between devices by JAX's collectives and lax.ppermute only.
A program may use at most 128 MiB of HBM per device.

```python
import math
import jax
import jax.numpy as jnp
from jax import lax

NFFT = 4096
MAXLAG = 1920
TAPS = 64
BAND = 64
CH_BLK = 8
NBLK = 4
REACH = 1
NOFF = 3
NCH = 32
NWIN = 16
RAW = 16384
HALF = 2048


def draw_records(key, part):
    scale_key = jax.random.fold_in(key, 11)
    envelope_key = jax.random.fold_in(key, 12)
    noise_key = jax.random.fold_in(key, 13)
    channel_scale = jnp.exp(jax.random.uniform(scale_key, (NCH, 1, 1, 1), jnp.float32) * math.log(10.0))
    envelope = jax.random.uniform(envelope_key, (NCH, NWIN, RAW // 512, 1), jnp.float32, 0.5, 2.0)
    noise = jax.random.normal(noise_key, (NCH, NWIN, RAW // 512, 512), jnp.float32)
    values = noise * envelope * channel_scale
    return jnp.clip(values, -32.0, 32.0).reshape(NCH, NWIN, RAW).astype(jnp.bfloat16)


def draw_segment_end(key, part):
    values = jax.random.randint(jax.random.fold_in(key, 21), (NWIN,), RAW // 2, RAW + 1)
    first_slot = jax.random.randint(jax.random.fold_in(key, 22), (), 0, NWIN)
    second_slot = (first_slot + jax.random.randint(jax.random.fold_in(key, 23), (), 1, NWIN)) % NWIN
    slots = jnp.arange(NWIN, dtype=jnp.int32)
    values = jnp.where(slots == first_slot, RAW, jnp.where(slots == second_slot, RAW // 2, values))
    return values.astype(jnp.int32)


def place_ends(array, rng, smallest, high):
    place = [jax.random.randint(jax.random.fold_in(rng, axis), (), 0, length) for axis, length in enumerate(array.shape)]
    widest = array.shape.index(max(array.shape))
    beside = place[:widest] + [(place[widest] + 1) % array.shape[widest]] + place[widest + 1:]
    return array.at[tuple(place)].set(smallest).at[tuple(beside)].set(high)


def bell_draw(stream_key, extent, scale, most, held_as=jnp.bfloat16):
    return jnp.clip(scale * jax.random.normal(stream_key, extent, jnp.float32), -most, most).astype(held_as)


def setup_inputs(seed: int = 0, part: int = 0) -> dict:
    key_of = jax.random.split(jax.random.key(seed), 5)
    own_keys = jax.random.split(jax.random.fold_in(key_of[4], part), 5)
    return {
        "records": draw_records(jax.random.fold_in(jax.random.fold_in(key_of[4], part), 71), part),
        "filter_taps": bell_draw(key_of[1], (TAPS,), TAPS ** -0.5, 0.75),
        "segment_end": draw_segment_end(jax.random.fold_in(jax.random.fold_in(key_of[4], part), 71), part),
        "pair_mask": place_ends((jax.random.randint(own_keys[3], (NBLK, NOFF), 0, 4) < 3).astype(jnp.int32), jax.random.fold_in(own_keys[3], 1), 0, 1),
    }


EPSILON = 1e-06

def reference(records, filter_taps, segment_end, pair_mask):
    kernel = filter_taps.astype(jnp.float32)[::-1].reshape(1, 1, TAPS)
    position = jnp.arange(RAW, dtype=jnp.int32)
    nonzero = (jnp.arange(HALF, dtype=jnp.int32) > 0).astype(jnp.float32)

    def whiten_channel(channel):
        retained = jnp.where(position[None, :] < segment_end[:, None], channel, jnp.zeros_like(channel))
        padded = jnp.pad(retained.astype(jnp.float32), ((0, 0), (TAPS - 4, 0)))
        filtered = lax.conv_general_dilated(padded[:, None, :], kernel, (4,), 'VALID', dimension_numbers=('NCH', 'OIH', 'NCH'), precision=lax.Precision.HIGHEST)[:, 0, :]
        rounded = lax.optimization_barrier(filtered.astype(jnp.bfloat16)).astype(jnp.float32)
        spectrum = jnp.fft.rfft(rounded, axis=-1)[:, :HALF]
        spec_re = jnp.real(spectrum).astype(jnp.float32)
        spec_im = jnp.imag(spectrum).astype(jnp.float32)
        energy = lax.optimization_barrier(jnp.mean((spec_re * spec_re + spec_im * spec_im).reshape(NWIN, HALF // BAND, BAND), axis=-1))
        divisor = jnp.repeat(jnp.sqrt(energy + EPSILON), BAND, axis=-1)
        white_re = (spec_re / divisor * nonzero).astype(jnp.bfloat16)
        white_im = (spec_im / divisor * nonzero).astype(jnp.bfloat16)
        return jnp.stack([white_re, white_im], axis=0)
    whitened = lax.map(whiten_channel, records)
    blocks = whitened.reshape(NBLK, CH_BLK, 2, NWIN, HALF)
    offsets = jnp.arange(NOFF, dtype=jnp.int32) - REACH
    scale = 1.0 / jnp.sqrt(jnp.float32(NWIN * HALF))

    def correlate_block(index):
        own_block = lax.dynamic_index_in_dim(blocks, index, 0, keepdims=False).astype(jnp.float32)
        partners = jnp.take(blocks, (index + offsets) % NBLK, axis=0).astype(jnp.float32)

        def contract(partner_part, own_part):
            return jnp.einsum('ojwf,iwf->ojif', partner_part, own_part, precision=lax.Precision.HIGHEST)
        real_part = contract(partners[:, :, 0], own_block[:, 0]) + contract(partners[:, :, 1], own_block[:, 1])
        imag_part = contract(partners[:, :, 0], own_block[:, 1]) - contract(partners[:, :, 1], own_block[:, 0])
        padded = jnp.pad(lax.complex(real_part, imag_part), ((0, 0), (0, 0), (0, 0), (0, NFFT - HALF)))
        circular = jnp.real(jnp.fft.ifft(padded, axis=-1)) * NFFT
        lagged = jnp.concatenate([circular[..., NFFT - MAXLAG:], circular[..., :MAXLAG]], axis=-1)
        weight = lax.dynamic_index_in_dim(pair_mask, index, 0, keepdims=False).astype(jnp.float32) * scale
        return (lagged * weight[:, None, None, None]).astype(jnp.float32)
    result = lax.map(correlate_block, jnp.arange(NBLK, dtype=jnp.int32))
    return jnp.transpose(result, (1, 2, 0, 3, 4)).reshape(NOFF, CH_BLK, NCH, 2 * MAXLAG)
```

```python
import functools
import math

import jax
import jax.numpy as jnp
import numpy as np
from jax import lax
from jax.experimental import pallas as pl
from jax.experimental.pallas import tpu as pltpu
from jax.sharding import PartitionSpec as P

MAXLAG = 1920
BAND = 64
EPSILON = 1e-06

LANES = 128
ROWS = 32
RESIDUES = ROWS // 2 + 1
BLOCK = 4 * LANES
SUB = 8
F32 = jnp.float32
BF16 = jnp.bfloat16
VMEM = pltpu.VMEM


def halves(table):
    high = table.astype(np.float32).astype(jnp.bfloat16)
    low = (table - high.astype(np.float64)).astype(np.float32).astype(jnp.bfloat16)
    return np.stack([high, low])


def forward_table():
    angle = 2.0 * np.pi / LANES * (np.outer(np.arange(LANES), np.arange(LANES)) % LANES)
    cos, sin = np.cos(angle), np.sin(angle)
    return halves(np.block([[cos, -sin], [sin, cos]]))


def inverse_table():
    angle = 2.0 * np.pi / LANES * (np.outer(np.arange(LANES), np.arange(LANES)) % LANES)
    cos, sin = np.cos(angle), np.sin(angle)
    return halves(np.block([[cos, sin], [-sin, cos]]))


def twist_table():
    angle = 2.0 * np.pi / (ROWS * LANES) * np.outer(np.arange(RESIDUES), np.arange(LANES))
    both = np.stack([np.cos(angle), np.sin(angle)]).astype(np.float32)
    return np.ascontiguousarray(np.broadcast_to(both[:, :, None, :], (2, RESIDUES, SUB, LANES)))


def band_table():
    place = np.arange(LANES)
    place = np.minimum(place, LANES - 1 - place)
    band = place // (BAND // ROWS)
    return (band[:, None] == band[None, :]).astype(np.float32).astype(jnp.bfloat16)


def turn(value, k, n):
    real, imag = value
    c, s = math.cos(2 * math.pi * k / n), math.sin(2 * math.pi * k / n)
    if 8 * k == n:
        return ((real + imag) * c, (imag - real) * c)
    if 8 * k == 3 * n:
        return ((imag - real) * s, -(real + imag) * s)
    return (real * c + imag * s, imag * c - real * s)


def real_transform(x):
    n = len(x)
    if n == 2:
        return [(x[0] + x[1], None), (x[0] - x[1], None)]
    even, odd = real_transform(x[0::2]), real_transform(x[1::2])
    out = [None] * (n // 2 + 1)
    out[0] = (even[0][0] + odd[0][0], None)
    out[n // 2] = (even[0][0] - odd[0][0], None)
    for k in range(1, n // 4):
        er, ei = even[k]
        tr, ti = turn(odd[k], k, n)
        out[k] = (er + tr, ei + ti)
        out[n // 2 - k] = (er - tr, ti - ei)
    out[n // 4] = (even[n // 4][0], -odd[n // 4][0])
    return out


def real_inverse(x):
    n = 2 * (len(x) - 1)
    if n == 2:
        return [x[0][0] + x[1][0], x[0][0] - x[1][0]]
    even, odd = [None] * (n // 4 + 1), [None] * (n // 4 + 1)
    even[0] = (x[0][0] + x[n // 2][0], None)
    odd[0] = (x[0][0] - x[n // 2][0], None)
    for k in range(1, n // 4):
        ar, ai = x[k]
        br, bi = x[n // 2 - k]
        even[k] = (ar + br, ai - bi)
        dr, di = turn((ar - br, -(ai + bi)), k, n)
        odd[k] = (dr, -di)
    even[n // 4] = (2.0 * x[n // 4][0], None)
    odd[n // 4] = (-2.0 * x[n // 4][1], None)
    a, b = real_inverse(even), real_inverse(odd)
    return [v for pair in zip(a, b) for v in pair]


def split(value):
    high = value.astype(BF16)
    return high, (value - high.astype(F32)).astype(BF16)


def three_pass(high, low, table_ref):
    def dot(a, b):
        return jnp.dot(a, b, preferred_element_type=F32)

    return dot(high, table_ref[0]) + dot(low, table_ref[0]) + dot(high, table_ref[1])


def decimate_kernel(place_ref, end_ref, base_ref, rec_ref, keep_ref, send_ref, lhs_ref):
    channels, windows, length = rec_ref.shape
    half = channels // 2
    rows = half * windows
    blocks = length // BLOCK
    tap_table = pltpu.roll(
        jnp.broadcast_to(base_ref[...], (LANES, BLOCK + LANES)), 0, 1, stride=4, stride_axis=0
    ).astype(BF16)
    row = lax.broadcasted_iota(jnp.int32, (windows, BLOCK), 0)
    lane = lax.broadcasted_iota(jnp.int32, (windows, BLOCK), 1)
    end = jnp.zeros((windows, BLOCK), jnp.int32)
    for w in range(windows):
        end = jnp.where(row == w, end_ref[w], end)
    end = end - place_ref[0] * length - lane
    for h, out_ref in ((0, keep_ref), (1, send_ref)):
        side = place_ref[1] if h == 0 else 1 - place_ref[1]
        lhs_ref[h, 0, :, 0:LANES] = jnp.zeros((rows, LANES), BF16)
        lhs_ref[h, blocks, :, LANES:] = jnp.zeros((rows, BLOCK), BF16)
        for b in range(blocks):
            x = rec_ref[pl.ds(side * half, half), :, b * BLOCK : (b + 1) * BLOCK].astype(F32)
            x = jnp.where((end > b * BLOCK)[None], x, 0.0)
            x = x.reshape(rows, BLOCK).astype(BF16)
            lhs_ref[h, b, :, LANES:] = x
            lhs_ref[h, b + 1, :, 0:LANES] = x[:, BLOCK - LANES :]
        out = lax.dot_general(
            lhs_ref[h].reshape((blocks + 1) * rows, BLOCK + LANES),
            tap_table,
            (((1,), (1,)), ((), ())),
            preferred_element_type=F32,
        )
        out_ref[...] = out.reshape(blocks + 1, half, windows, LANES).astype(BF16)


def decimate(records, filter_taps, segment_end, place):
    channels, windows, length = records.shape
    taps = filter_taps.shape[0]
    reverse = filter_taps.astype(F32)[::-1]
    base = jnp.pad(reverse, (LANES + 4 - taps, BLOCK - 4)).reshape(1, BLOCK + LANES)
    blocks = length // BLOCK
    piece = jax.ShapeDtypeStruct((blocks + 1, channels // 2, windows, LANES), BF16)
    return pl.pallas_call(
        decimate_kernel,
        out_shape=(piece, piece),
        in_specs=[
            pl.BlockSpec(memory_space=pltpu.SMEM),
            pl.BlockSpec(memory_space=pltpu.SMEM),
            pl.BlockSpec(memory_space=VMEM),
            pl.BlockSpec(memory_space=VMEM),
        ],
        out_specs=(pl.BlockSpec(memory_space=VMEM),) * 2,
        scratch_shapes=[VMEM((2, blocks + 1, channels // 2 * windows, BLOCK + LANES), BF16)],
        compiler_params=pltpu.CompilerParams(vmem_limit_bytes=24 << 20),
        cost_estimate=pl.CostEstimate(
            flops=2 * records.size // 4 * BLOCK, bytes_accessed=3 * records.size, transcendentals=0
        ),
        name="decimate",
    )(place, segment_end, base, records)


def spectra(segments, flags, tables, work, store):
    twist_ref, dft_ref, band_ref = tables
    high_ref, low_ref, spec_ref, power_ref = work
    depth, groups = segments[0].shape[0] - 1, segments[0].shape[1]

    def first(g, carry):
        x = []
        for s in range(len(segments)):
            for r in range(depth):
                value = segments[s][r, g].astype(F32)
                if r == 0:
                    value = value + segments[s - 1][depth, g].astype(F32) * flags[s]
                x.append(value)
        for q, (real, imag) in enumerate(real_transform(x)):
            if q == 0:
                turned = (real, jnp.zeros_like(real))
            else:
                cos, sin = twist_ref[0, q], twist_ref[1, q]
                if imag is None:
                    turned = (real * cos, -(real * sin))
                else:
                    turned = (real * cos + imag * sin, imag * cos - real * sin)
            for part in range(2):
                high, low = split(turned[part])
                high_ref[g, q, :, part * LANES : (part + 1) * LANES] = high
                low_ref[g, q, :, part * LANES : (part + 1) * LANES] = low
        return carry

    lax.fori_loop(0, groups, first, 0)
    count = groups * RESIDUES * SUB
    spec = three_pass(
        high_ref[...].reshape(count, 2 * LANES), low_ref[...].reshape(count, 2 * LANES), dft_ref
    )
    spec_ref[...] = spec.reshape(groups, RESIDUES, SUB, 2 * LANES)
    lower = (lax.broadcasted_iota(jnp.int32, (SUB, LANES), 1) < LANES // 2).astype(F32)

    def powers(g, carry):
        ends = inner = None
        for q in range(RESIDUES):
            real, imag = spec_ref[g, q, :, :LANES], spec_ref[g, q, :, LANES:]
            power = real * real + imag * imag
            if q in (0, RESIDUES - 1):
                ends = power if ends is None else ends + power
            else:
                inner = power if inner is None else inner + power
        power_ref[g] = inner + ends * lower
        return carry

    lax.fori_loop(0, groups, powers, 0)
    high, low = split(power_ref[...].reshape(groups * SUB, LANES))
    energy = jnp.dot(high, band_ref[...], preferred_element_type=F32) + jnp.dot(
        low, band_ref[...], preferred_element_type=F32
    )
    power_ref[...] = lax.rsqrt(energy * (1.0 / BAND) + EPSILON).reshape(groups, SUB, LANES)
    lane = lax.broadcasted_iota(jnp.int32, (SUB, LANES), 1)
    nonzero = (lane > 0).astype(F32)

    def whiten(g, carry):
        scale = power_ref[g]
        for q in range(RESIDUES):
            factor = scale
            if q == 0:
                factor = scale * lower * nonzero
            elif q == RESIDUES - 1:
                factor = scale * lower
            for part in range(2):
                value = spec_ref[g, q, :, part * LANES : (part + 1) * LANES]
                store(part, g, q, (value * factor).astype(BF16))
        return carry

    lax.fori_loop(0, groups, whiten, 0)


def gather_rows(values):
    row = lax.broadcasted_iota(jnp.int32, (SUB, LANES), 0)
    step = SUB // 2
    while step:
        lower = (row % (2 * step)) < step
        values = [
            jnp.where(lower, a, b) + pltpu.roll(jnp.where(lower, b, a), step, 0)
            if step == SUB // 2
            else jnp.where(lower, a, b) + swap(jnp.where(lower, b, a), step, lower)
            for a, b in zip(values[:step], values[step:])
        ]
        step //= 2
    return values[0]


def swap(value, step, lower):
    return jnp.where(lower, pltpu.roll(value, SUB - step, 0), pltpu.roll(value, step, 0))


def correlate(own_load, remote_load, chunks, owned, remotes, tables, work, weight, lag_ref):
    twist_ref, inverse_ref = tables
    high_ref, low_ref, sum_ref = work
    pair_groups = remotes * owned // SUB

    def cross(q, carry):
        own = [[[own_load(c, p, i, q).astype(F32) for p in range(2)] for i in range(owned)] for c in range(chunks)]
        for group in range(pair_groups):
            real, imag = [], []
            for pair in range(group * SUB, (group + 1) * SUB):
                j, i = pair // owned, pair % owned
                re = im = None
                for c in range(chunks):
                    ar, ai = own[c][i]
                    br, bi = (remote_load(c, p, j, q).astype(F32) for p in range(2))
                    r = ar * br + ai * bi
                    m = ai * br - ar * bi
                    re = r if re is None else re + r
                    im = m if im is None else im + m
                real.append(re)
                imag.append(im)
            for part, values in enumerate((real, imag)):
                high, low = split(gather_rows(values))
                high_ref[group, q, :, part * LANES : (part + 1) * LANES] = high
                low_ref[group, q, :, part * LANES : (part + 1) * LANES] = low
        return carry

    lax.fori_loop(0, RESIDUES, cross, 0)
    count = pair_groups * RESIDUES * SUB
    total = three_pass(
        high_ref[...].reshape(count, 2 * LANES), low_ref[...].reshape(count, 2 * LANES), inverse_ref
    )
    sum_ref[...] = total.reshape(pair_groups, RESIDUES, SUB, 2 * LANES)
    lag_rows = MAXLAG // LANES
    per = SUB // owned

    def lags(group, carry):
        x = []
        for q in range(RESIDUES):
            real, imag = sum_ref[group, q, :, :LANES], sum_ref[group, q, :, LANES:]
            if q == 0:
                x.append((real, None))
                continue
            cos, sin = twist_ref[0, q], twist_ref[1, q]
            turned = real * cos - imag * sin
            if q == RESIDUES - 1:
                x.append((turned, None))
            else:
                x.append((0.5 * turned, 0.5 * (real * sin + imag * cos)))
        out = real_inverse(x)
        for place, a in enumerate((*range(ROWS - lag_rows, ROWS), *range(lag_rows))):
            value = out[a] * weight
            for j in range(per):
                lag_ref[group * per + j, :, place * LANES : (place + 1) * LANES] = value[
                    j * owned : (j + 1) * owned
                ]
        return carry

    lax.fori_loop(0, pair_groups, lags, 0)


def write_out(lag_ref, out_ref, offset, sem):
    copy = pltpu.make_async_copy(lag_ref, out_ref.at[offset], sem)
    copy.start()
    copy.wait()


def flags_of(place_ref, span):
    t = place_ref[0]
    return [((t + s) % span != 0).astype(F32) for s in range(span)]


def whiten_kernel(span, place_ref, *refs):
    pieces = refs[: 2 * span]
    twist_ref, dft_ref, band_ref, white_ref = refs[2 * span : 2 * span + 4]
    work = refs[2 * span + 4 :]
    flags = flags_of(place_ref, span)
    for c in range(2):

        def store(part, g, q, value, c=c):
            white_ref[c, part, g, q] = value

        spectra(pieces[c * span : (c + 1) * span], flags, (twist_ref, dft_ref, band_ref), work, store)


def own_pairs_kernel(
    owned, offset, scale, place_ref, mask_ref, white_ref, other_ref, twist_ref, inverse_ref,
    own_ref, out_ref, high_ref, low_ref, sum_ref, lag_ref, sem,
):
    groups = white_ref.shape[2]
    first = place_ref[0] * owned
    inside = lax.rem(first, groups)
    here = lax.div(first, groups) == place_ref[1]

    @pl.when(here)
    def _():
        own_ref[...] = white_ref[:, :, pl.ds(inside, owned)]

    @pl.when(jnp.logical_not(here))
    def _():
        for c in range(2):
            own_ref[c] = other_ref[1 - c, :, pl.ds(inside, owned)]

    correlate(
        lambda c, p, i, q: own_ref[c, p, i, q],
        lambda c, p, j, q: white_ref[c, p, j, q],
        2, owned, groups, (twist_ref, inverse_ref), (high_ref, low_ref, sum_ref),
        mask_ref[0, offset].astype(F32) * scale, lag_ref,
    )
    write_out(lag_ref, out_ref, offset, sem)


def far_pairs_kernel(span, owned, offset, scale, place_ref, mask_ref, *refs):
    pieces = refs[: 2 * span]
    own_ref, twist_ref, dft_ref, band_ref, inverse_ref, _, out_ref = refs[2 * span : 2 * span + 7]
    (
        white_ref, zhigh_ref, zlow_ref, spec_ref, power_ref, high_ref, low_ref, sum_ref, lag_ref, sem,
    ) = refs[2 * span + 7 :]
    flags = flags_of(place_ref, span)
    groups = white_ref.shape[2]
    for c in range(2):

        def store(part, g, q, value, c=c):
            white_ref[c, part, g, q] = value

        spectra(
            pieces[c * span : (c + 1) * span], flags, (twist_ref, dft_ref, band_ref),
            (zhigh_ref, zlow_ref, spec_ref, power_ref), store,
        )
    correlate(
        lambda c, p, i, q: own_ref[c, p, i, q],
        lambda c, p, j, q: white_ref[c, p, j, q],
        2, owned, groups, (twist_ref, inverse_ref), (high_ref, low_ref, sum_ref),
        mask_ref[0, offset].astype(F32) * scale, lag_ref,
    )
    write_out(lag_ref, out_ref, offset, sem)


def spectra_work(groups):
    return [
        VMEM((groups, RESIDUES, SUB, 2 * LANES), BF16),
        VMEM((groups, RESIDUES, SUB, 2 * LANES), BF16),
        VMEM((groups, RESIDUES, SUB, 2 * LANES), F32),
        VMEM((groups, SUB, LANES), F32),
    ]


def lag_work(groups, owned):
    pair_groups = groups * owned // SUB
    return [
        VMEM((pair_groups, RESIDUES, SUB, 2 * LANES), BF16),
        VMEM((pair_groups, RESIDUES, SUB, 2 * LANES), BF16),
        VMEM((pair_groups, RESIDUES, SUB, 2 * LANES), F32),
        VMEM((groups, owned, 2 * MAXLAG), F32),
        pltpu.SemaphoreType.DMA,
    ]


def params(microseconds):
    return dict(
        compiler_params=pltpu.CompilerParams(vmem_limit_bytes=16 << 20),
        cost_estimate=pl.CostEstimate(
            flops=int(microseconds * 1e9), bytes_accessed=1 << 20, transcendentals=0
        ),
    )


def shards(records, filter_taps, segment_end, pair_mask):
    span = lax.axis_size("tm")
    owned = records.shape[0] // span
    groups = records.shape[0] // 2
    reach = (pair_mask.shape[1] - 1) // 2
    windows = 2 * records.shape[1]
    scale = 1.0 / math.sqrt(windows * ROWS * LANES // 2)
    place = jnp.stack([lax.axis_index("tm"), lax.axis_index("win")]).astype(jnp.int32)
    twist, dft, inverse, band = (
        jnp.asarray(t) for t in (twist_table(), forward_table(), inverse_table(), band_table())
    )
    smem, vmem = pl.BlockSpec(memory_space=pltpu.SMEM), pl.BlockSpec(memory_space=VMEM)
    anywhere = pl.BlockSpec(memory_space=pl.ANY)

    def permute(array, axis, by):
        count = lax.axis_size(axis)
        return lax.ppermute(array, axis, [(i, (i + by) % count) for i in range(count)])

    def segments(chunk):
        return [chunk] + [permute(chunk, "tm", -s) for s in range(1, span)]

    keep, send = decimate(records, filter_taps, segment_end, place)
    chunks = [keep, permute(send, "win", 1)]
    up = down = chunks
    moved = []
    for _ in range(reach):
        up = [permute(chunk, "chan", 1) for chunk in up]
        down = [permute(chunk, "chan", -1) for chunk in down]
        moved.append((up, down))
    white = pl.pallas_call(
        functools.partial(whiten_kernel, span),
        out_shape=jax.ShapeDtypeStruct((2, 2, groups, RESIDUES, SUB, LANES), BF16),
        in_specs=[smem] + [vmem] * (2 * span + 3),
        out_specs=vmem,
        scratch_shapes=spectra_work(groups),
        name="whiten",
        **params(3),
    )(place, *segments(chunks[0]), *segments(chunks[1]), twist, dft, band)
    other = permute(white, "win", 1)
    own, out = pl.pallas_call(
        functools.partial(own_pairs_kernel, owned, reach, scale),
        out_shape=(
            jax.ShapeDtypeStruct((2, 2, owned, RESIDUES, SUB, LANES), BF16),
            jax.ShapeDtypeStruct((2 * reach + 1, groups, owned, 2 * MAXLAG), F32),
        ),
        in_specs=[smem, smem] + [vmem] * 4,
        out_specs=(vmem, anywhere),
        scratch_shapes=lag_work(groups, owned),
        name="own_pairs",
        **params(2),
    )(place, pair_mask, white, other, twist, inverse)
    for step, sides in enumerate(moved):
        for side, far in zip((-1, 1), sides):
            offset = reach + side * (step + 1)
            out = pl.pallas_call(
                functools.partial(far_pairs_kernel, span, owned, offset, scale),
                out_shape=jax.ShapeDtypeStruct(out.shape, out.dtype),
                in_specs=[smem, smem] + [vmem] * (2 * span + 5) + [anywhere],
                out_specs=anywhere,
                scratch_shapes=[VMEM((2, 2, groups, RESIDUES, SUB, LANES), BF16)]
                + spectra_work(groups)
                + lag_work(groups, owned),
                input_output_aliases={2 * span + 7: 0},
                name="far_pairs",
                **params(4),
            )(place, pair_mask, *segments(far[0]), *segments(far[1]), own, twist, dft, band, inverse, out)
    return out


def solution(mesh):
    placed = (
        P(("fibre", "chan"), "win", "tm"),
        P(),
        P(("fibre", "win")),
        P(("fibre", "chan"), None),
    )
    return jax.shard_map(
        shards,
        mesh=mesh,
        in_specs=placed,
        out_specs=P(None, "win", ("fibre", "chan", "tm"), None),
        check_vma=False,
    )
```

```python
import functools
import math

import jax
import jax.numpy as jnp
import numpy as np
from jax import lax
from jax.experimental import pallas as pl
from jax.experimental.pallas import tpu as pltpu
from jax.sharding import PartitionSpec as P

MAXLAG = 1920
BAND = 64
EPSILON = 1e-06

LANES = 128
ROWS = 32
RESIDUES = ROWS // 2 + 1
BLOCK = 4 * LANES
SUB = 8
F32 = jnp.float32
BF16 = jnp.bfloat16
VMEM = pltpu.VMEM


def halves(table):
    high = table.astype(np.float32).astype(jnp.bfloat16)
    low = (table - high.astype(np.float64)).astype(np.float32).astype(jnp.bfloat16)
    return np.stack([high, low])


def forward_table():
    angle = 2.0 * np.pi / LANES * (np.outer(np.arange(LANES), np.arange(LANES)) % LANES)
    cos, sin = np.cos(angle), np.sin(angle)
    return halves(np.block([[cos, -sin], [sin, cos]]))


def inverse_table():
    angle = 2.0 * np.pi / LANES * (np.outer(np.arange(LANES), np.arange(LANES)) % LANES)
    cos, sin = np.cos(angle), np.sin(angle)
    return halves(np.block([[cos, sin], [-sin, cos]]))


def twist_table():
    angle = 2.0 * np.pi / (ROWS * LANES) * np.outer(np.arange(RESIDUES), np.arange(LANES))
    both = np.stack([np.cos(angle), np.sin(angle)]).astype(np.float32)
    return np.ascontiguousarray(np.broadcast_to(both[:, :, None, :], (2, RESIDUES, SUB, LANES)))


def band_table():
    place = np.arange(LANES)
    place = np.minimum(place, LANES - 1 - place)
    band = place // (BAND // ROWS)
    return (band[:, None] == band[None, :]).astype(np.float32).astype(jnp.bfloat16)


def turn(value, k, n):
    real, imag = value
    c, s = math.cos(2 * math.pi * k / n), math.sin(2 * math.pi * k / n)
    if 8 * k == n:
        return ((real + imag) * c, (imag - real) * c)
    if 8 * k == 3 * n:
        return ((imag - real) * s, -(real + imag) * s)
    return (real * c + imag * s, imag * c - real * s)


def real_transform(x):
    n = len(x)
    if n == 2:
        return [(x[0] + x[1], None), (x[0] - x[1], None)]
    even, odd = real_transform(x[0::2]), real_transform(x[1::2])
    out = [None] * (n // 2 + 1)
    out[0] = (even[0][0] + odd[0][0], None)
    out[n // 2] = (even[0][0] - odd[0][0], None)
    for k in range(1, n // 4):
        er, ei = even[k]
        tr, ti = turn(odd[k], k, n)
        out[k] = (er + tr, ei + ti)
        out[n // 2 - k] = (er - tr, ti - ei)
    out[n // 4] = (even[n // 4][0], -odd[n // 4][0])
    return out


def real_inverse(x):
    n = 2 * (len(x) - 1)
    if n == 2:
        return [x[0][0] + x[1][0], x[0][0] - x[1][0]]
    even, odd = [None] * (n // 4 + 1), [None] * (n // 4 + 1)
    even[0] = (x[0][0] + x[n // 2][0], None)
    odd[0] = (x[0][0] - x[n // 2][0], None)
    for k in range(1, n // 4):
        ar, ai = x[k]
        br, bi = x[n // 2 - k]
        even[k] = (ar + br, ai - bi)
        dr, di = turn((ar - br, -(ai + bi)), k, n)
        odd[k] = (dr, -di)
    even[n // 4] = (2.0 * x[n // 4][0], None)
    odd[n // 4] = (-2.0 * x[n // 4][1], None)
    a, b = real_inverse(even), real_inverse(odd)
    return [v for pair in zip(a, b) for v in pair]


def split(value):
    high = value.astype(BF16)
    return high, (value - high.astype(F32)).astype(BF16)


def three_pass(high, low, table_ref):
    def dot(a, b):
        return jnp.dot(a, b, preferred_element_type=F32)

    return dot(high, table_ref[0]) + dot(low, table_ref[0]) + dot(high, table_ref[1])


def decimate_kernel(
    place_ref, end_hbm, taps_hbm, rec_hbm, keep_ref, send_ref,
    rec_ref, lhs_ref, taps_ref, end_ref, rec_sem, small_sem,
):
    channels, windows, length = rec_ref.shape
    half = channels // 2
    rows = half * windows
    blocks = length // BLOCK
    pieces = rec_sem.shape[0]
    piece = length // pieces
    taps = taps_hbm.shape[1]
    small = [
        pltpu.make_async_copy(end_hbm, end_ref, small_sem.at[0]),
        pltpu.make_async_copy(taps_hbm, taps_ref, small_sem.at[1]),
    ]
    copies = [
        pltpu.make_async_copy(
            rec_hbm.at[:, :, k * piece : (k + 1) * piece],
            rec_ref.at[:, :, k * piece : (k + 1) * piece],
            rec_sem.at[k],
        )
        for k in range(pieces)
    ]
    for copy in small + copies:
        copy.start()
    row = lax.broadcasted_iota(jnp.int32, (windows, BLOCK), 0)
    lane = lax.broadcasted_iota(jnp.int32, (windows, BLOCK), 1)
    tap = lax.broadcasted_iota(jnp.int32, (taps, BLOCK + LANES), 0)
    at = lax.broadcasted_iota(jnp.int32, (taps, BLOCK + LANES), 1)
    chosen = jnp.where(tap + at == LANES + 3, 1.0, 0.0).astype(BF16)
    for copy in small:
        copy.wait()
    base = jnp.dot(
        jnp.broadcast_to(taps_ref[...].astype(F32), (SUB, taps)).astype(BF16), chosen,
        preferred_element_type=F32,
    )
    tap_table = pltpu.roll(
        jnp.broadcast_to(base[0:1], (LANES, BLOCK + LANES)), 0, 1, stride=4, stride_axis=0
    ).astype(BF16)
    end = jnp.zeros((windows, BLOCK), jnp.int32)
    for w in range(windows):
        end = jnp.where(row == w, end_ref[w], end)
    end = end - place_ref[0] * length - lane
    for h in range(2):
        lhs_ref[h, 0, :, 0:LANES] = jnp.zeros((rows, LANES), BF16)
        lhs_ref[h, blocks, :, LANES:] = jnp.zeros((rows, BLOCK), BF16)
    for b in range(blocks):
        if b * BLOCK % piece == 0:
            copies[b * BLOCK // piece].wait()
        for h in range(2):
            side = place_ref[1] if h == 0 else 1 - place_ref[1]
            x = rec_ref[pl.ds(side * half, half), :, b * BLOCK : (b + 1) * BLOCK].astype(F32)
            x = jnp.where((end > b * BLOCK)[None], x, 0.0)
            x = x.reshape(rows, BLOCK).astype(BF16)
            lhs_ref[h, b, :, LANES:] = x
            lhs_ref[h, b + 1, :, 0:LANES] = x[:, BLOCK - LANES :]
    for h, out_ref in ((0, keep_ref), (1, send_ref)):
        out = lax.dot_general(
            lhs_ref[h].reshape((blocks + 1) * rows, BLOCK + LANES),
            tap_table,
            (((1,), (1,)), ((), ())),
            preferred_element_type=F32,
        )
        out_ref[...] = out.reshape(blocks + 1, half, windows, LANES).astype(BF16)


def decimate(records, filter_taps, segment_end, place):
    channels, windows, length = records.shape
    blocks = length // BLOCK
    piece = jax.ShapeDtypeStruct((blocks + 1, channels // 2, windows, LANES), BF16)
    return pl.pallas_call(
        decimate_kernel,
        out_shape=(piece, piece),
        in_specs=[pl.BlockSpec(memory_space=pltpu.SMEM)] + [pl.BlockSpec(memory_space=pltpu.HBM)] * 3,
        out_specs=(pl.BlockSpec(memory_space=VMEM),) * 2,
        scratch_shapes=[
            VMEM(records.shape, BF16),
            VMEM((2, blocks + 1, channels // 2 * windows, BLOCK + LANES), BF16),
            VMEM((1, filter_taps.shape[0]), BF16),
            pltpu.SMEM(segment_end.shape, jnp.int32),
            pltpu.SemaphoreType.DMA((4,)),
            pltpu.SemaphoreType.DMA((2,)),
        ],
        compiler_params=pltpu.CompilerParams(vmem_limit_bytes=24 << 20),
        cost_estimate=pl.CostEstimate(
            flops=2 * records.size // 4 * BLOCK, bytes_accessed=3 * records.size, transcendentals=0
        ),
        name="decimate",
    )(place, *(pltpu.with_memory_space_constraint(a, pltpu.HBM) for a in (segment_end, filter_taps.reshape(1, -1), records)))


def join_kernel(first_ref, second_ref, out_ref):
    out_ref[0] = first_ref[...]
    out_ref[1] = second_ref[...]


def join(first, second):
    vmem = pl.BlockSpec(memory_space=VMEM)
    return pl.pallas_call(
        join_kernel,
        out_shape=jax.ShapeDtypeStruct((2, *first.shape), first.dtype),
        in_specs=[vmem, vmem],
        out_specs=vmem,
        name="join",
        **params(0.2),
    )(first, second)


def spectra(segments, flags, tables, work, store):
    twist_ref, dft_ref, band_ref = tables
    high_ref, low_ref, spec_ref, power_ref = work
    depth, groups = segments[0].shape[0] - 1, segments[0].shape[1]

    def first(g, carry):
        x = []
        for s in range(len(segments)):
            for r in range(depth):
                value = segments[s][r, g].astype(F32)
                if r == 0:
                    value = value + segments[s - 1][depth, g].astype(F32) * flags[s]
                x.append(value)
        for q, (real, imag) in enumerate(real_transform(x)):
            if q == 0:
                turned = (real, jnp.zeros_like(real))
            else:
                cos, sin = twist_ref[0, q], twist_ref[1, q]
                if imag is None:
                    turned = (real * cos, -(real * sin))
                else:
                    turned = (real * cos + imag * sin, imag * cos - real * sin)
            for part in range(2):
                high, low = split(turned[part])
                high_ref[g, q, :, part * LANES : (part + 1) * LANES] = high
                low_ref[g, q, :, part * LANES : (part + 1) * LANES] = low
        return carry

    lax.fori_loop(0, groups, first, 0, unroll=True)
    count = groups * RESIDUES * SUB
    spec = three_pass(
        high_ref[...].reshape(count, 2 * LANES), low_ref[...].reshape(count, 2 * LANES), dft_ref
    )
    spec_ref[...] = spec.reshape(groups, RESIDUES, SUB, 2 * LANES)
    lower = (lax.broadcasted_iota(jnp.int32, (SUB, LANES), 1) < LANES // 2).astype(F32)

    def powers(g, carry):
        ends = inner = None
        for q in range(RESIDUES):
            real, imag = spec_ref[g, q, :, :LANES], spec_ref[g, q, :, LANES:]
            power = real * real + imag * imag
            if q in (0, RESIDUES - 1):
                ends = power if ends is None else ends + power
            else:
                inner = power if inner is None else inner + power
        power_ref[g] = inner + ends * lower
        return carry

    lax.fori_loop(0, groups, powers, 0, unroll=True)
    high, low = split(power_ref[...].reshape(groups * SUB, LANES))
    energy = jnp.dot(high, band_ref[...], preferred_element_type=F32) + jnp.dot(
        low, band_ref[...], preferred_element_type=F32
    )
    power_ref[...] = lax.rsqrt(energy * (1.0 / BAND) + EPSILON).reshape(groups, SUB, LANES)
    lane = lax.broadcasted_iota(jnp.int32, (SUB, LANES), 1)
    nonzero = (lane > 0).astype(F32)

    def whiten(g, carry):
        scale = power_ref[g]
        for q in range(RESIDUES):
            factor = scale
            if q == 0:
                factor = scale * lower * nonzero
            elif q == RESIDUES - 1:
                factor = scale * lower
            for part in range(2):
                value = spec_ref[g, q, :, part * LANES : (part + 1) * LANES]
                store(part, g, q, (value * factor).astype(BF16))
        return carry

    lax.fori_loop(0, groups, whiten, 0, unroll=True)


def gather_rows(values):
    row = lax.broadcasted_iota(jnp.int32, (SUB, LANES), 0)
    step = SUB // 2
    while step:
        lower = (row % (2 * step)) < step
        values = [
            jnp.where(lower, a, b) + pltpu.roll(jnp.where(lower, b, a), step, 0)
            if step == SUB // 2
            else jnp.where(lower, a, b) + swap(jnp.where(lower, b, a), step, lower)
            for a, b in zip(values[:step], values[step:])
        ]
        step //= 2
    return values[0]


def swap(value, step, lower):
    return jnp.where(lower, pltpu.roll(value, SUB - step, 0), pltpu.roll(value, step, 0))


def correlate(own_load, remote_load, chunks, owned, remotes, tables, work, weight, lag_ref):
    twist_ref, inverse_ref = tables
    high_ref, low_ref, sum_ref = work
    pair_groups = remotes * owned // SUB

    def cross(q, carry):
        own = [[[own_load(c, p, i, q).astype(F32) for p in range(2)] for i in range(owned)] for c in range(chunks)]
        for group in range(pair_groups):
            real, imag = [], []
            for pair in range(group * SUB, (group + 1) * SUB):
                j, i = pair // owned, pair % owned
                re = im = None
                for c in range(chunks):
                    ar, ai = own[c][i]
                    br, bi = (remote_load(c, p, j, q).astype(F32) for p in range(2))
                    r = ar * br + ai * bi
                    m = ai * br - ar * bi
                    re = r if re is None else re + r
                    im = m if im is None else im + m
                real.append(re)
                imag.append(im)
            for part, values in enumerate((real, imag)):
                high, low = split(gather_rows(values))
                high_ref[group, q, :, part * LANES : (part + 1) * LANES] = high
                low_ref[group, q, :, part * LANES : (part + 1) * LANES] = low
        return carry

    lax.fori_loop(0, RESIDUES, cross, 0, unroll=True)
    count = pair_groups * RESIDUES * SUB
    total = three_pass(
        high_ref[...].reshape(count, 2 * LANES), low_ref[...].reshape(count, 2 * LANES), inverse_ref
    )
    sum_ref[...] = total.reshape(pair_groups, RESIDUES, SUB, 2 * LANES)
    lag_rows = MAXLAG // LANES
    per = SUB // owned

    def lags(group, carry):
        x = []
        for q in range(RESIDUES):
            real, imag = sum_ref[group, q, :, :LANES], sum_ref[group, q, :, LANES:]
            if q == 0:
                x.append((real, None))
                continue
            cos, sin = twist_ref[0, q], twist_ref[1, q]
            turned = real * cos - imag * sin
            if q == RESIDUES - 1:
                x.append((turned, None))
            else:
                x.append((0.5 * turned, 0.5 * (real * sin + imag * cos)))
        out = real_inverse(x)
        for place, a in enumerate((*range(ROWS - lag_rows, ROWS), *range(lag_rows))):
            value = out[a] * weight
            for j in range(per):
                lag_ref[group * per + j, :, place * LANES : (place + 1) * LANES] = value[
                    j * owned : (j + 1) * owned
                ]
        return carry

    lax.fori_loop(0, pair_groups, lags, 0, unroll=True)


def write_out(lag_ref, out_ref, offset, sem):
    copy = pltpu.make_async_copy(lag_ref, out_ref.at[offset], sem)
    copy.start()
    copy.wait()


def flags_of(place_ref, span):
    t = place_ref[0]
    return [((t + s) % span != 0).astype(F32) for s in range(span)]


def whiten_kernel(span, place_ref, *refs):
    pieces = refs[:span]
    twist_ref, dft_ref, band_ref = refs[span : span + 3]
    white_refs = refs[span + 3 : span + 5]
    work = refs[span + 5 :]
    flags = flags_of(place_ref, span)
    for c in range(2):

        def store(part, g, q, value, c=c):
            white_refs[c][part, g, q] = value

        spectra([piece.at[c] for piece in pieces], flags, (twist_ref, dft_ref, band_ref), work, store)


def own_pairs_kernel(
    owned, offset, scale, place_ref, mask_ref, *refs,
):
    white_refs, other_refs = refs[:2], refs[2:4]
    twist_ref, inverse_ref, own_ref, out_ref, high_ref, low_ref, sum_ref, lag_ref, sem = refs[4:]
    groups = white_refs[0].shape[1]
    first = place_ref[0] * owned
    inside = lax.rem(first, groups)
    here = lax.div(first, groups) == place_ref[1]

    @pl.when(here)
    def _():
        for c in range(2):
            own_ref[c] = white_refs[c][:, pl.ds(inside, owned)]

    @pl.when(jnp.logical_not(here))
    def _():
        for c in range(2):
            own_ref[c] = other_refs[1 - c][:, pl.ds(inside, owned)]

    correlate(
        lambda c, p, i, q: own_ref[c, p, i, q],
        lambda c, p, j, q: white_refs[c][p, j, q],
        2, owned, groups, (twist_ref, inverse_ref), (high_ref, low_ref, sum_ref),
        mask_ref[0, offset].astype(F32) * scale, lag_ref,
    )
    write_out(lag_ref, out_ref, offset, sem)


def far_pairs_kernel(span, owned, offset, scale, place_ref, mask_ref, *refs):
    pieces = refs[:span]
    own_ref, twist_ref, dft_ref, band_ref, inverse_ref, _, out_ref = refs[span : span + 7]
    (
        white_ref, zhigh_ref, zlow_ref, spec_ref, power_ref, high_ref, low_ref, sum_ref, lag_ref, sem,
    ) = refs[span + 7 :]
    flags = flags_of(place_ref, span)
    groups = white_ref.shape[2]
    for c in range(2):

        def store(part, g, q, value, c=c):
            white_ref[c, part, g, q] = value

        spectra(
            [piece.at[c] for piece in pieces], flags, (twist_ref, dft_ref, band_ref),
            (zhigh_ref, zlow_ref, spec_ref, power_ref), store,
        )
    correlate(
        lambda c, p, i, q: own_ref[c, p, i, q],
        lambda c, p, j, q: white_ref[c, p, j, q],
        2, owned, groups, (twist_ref, inverse_ref), (high_ref, low_ref, sum_ref),
        mask_ref[0, offset].astype(F32) * scale, lag_ref,
    )
    write_out(lag_ref, out_ref, offset, sem)


def spectra_work(groups):
    return [
        VMEM((groups, RESIDUES, SUB, 2 * LANES), BF16),
        VMEM((groups, RESIDUES, SUB, 2 * LANES), BF16),
        VMEM((groups, RESIDUES, SUB, 2 * LANES), F32),
        VMEM((groups, SUB, LANES), F32),
    ]


def lag_work(groups, owned):
    pair_groups = groups * owned // SUB
    return [
        VMEM((pair_groups, RESIDUES, SUB, 2 * LANES), BF16),
        VMEM((pair_groups, RESIDUES, SUB, 2 * LANES), BF16),
        VMEM((pair_groups, RESIDUES, SUB, 2 * LANES), F32),
        VMEM((groups, owned, 2 * MAXLAG), F32),
        pltpu.SemaphoreType.DMA,
    ]


def params(microseconds):
    return dict(
        compiler_params=pltpu.CompilerParams(vmem_limit_bytes=16 << 20),
        cost_estimate=pl.CostEstimate(
            flops=int(microseconds * 1e6), bytes_accessed=1 << 10, transcendentals=0
        ),
    )


def shards(records, filter_taps, segment_end, pair_mask):
    span = lax.axis_size("tm")
    owned = records.shape[0] // span
    groups = records.shape[0] // 2
    reach = (pair_mask.shape[1] - 1) // 2
    windows = 2 * records.shape[1]
    scale = 1.0 / math.sqrt(windows * ROWS * LANES // 2)
    place = jnp.stack([lax.axis_index("tm"), lax.axis_index("win")]).astype(jnp.int32)
    twist, dft, inverse, band = (
        jnp.asarray(t) for t in (twist_table(), forward_table(), inverse_table(), band_table())
    )
    smem, vmem = pl.BlockSpec(memory_space=pltpu.SMEM), pl.BlockSpec(memory_space=VMEM)
    anywhere = pl.BlockSpec(memory_space=pl.ANY)

    def permute(array, axis, by):
        count = lax.axis_size(axis)
        return lax.ppermute(array, axis, [(i, (i + by) % count) for i in range(count)])

    def segments(chunk):
        return [chunk] + [permute(chunk, "tm", -s) for s in range(1, span)]

    keep, send = decimate(records, filter_taps, segment_end, place)
    block = join(keep, permute(send, "win", 1))
    up = down = block
    moved = []
    for _ in range(reach):
        up, down = permute(up, "chan", 1), permute(down, "chan", -1)
        moved.append([up, down])
    mine = segments(block)
    white = pl.pallas_call(
        functools.partial(whiten_kernel, span),
        out_shape=(jax.ShapeDtypeStruct((2, groups, RESIDUES, SUB, LANES), BF16),) * 2,
        in_specs=[smem] + [vmem] * (span + 3),
        out_specs=(vmem,) * 2,
        scratch_shapes=spectra_work(groups),
        name="whiten",
        **params(3),
    )(place, *mine, twist, dft, band)
    other = [permute(part, "win", 1) for part in white]
    own, out = pl.pallas_call(
        functools.partial(own_pairs_kernel, owned, reach, scale),
        out_shape=(
            jax.ShapeDtypeStruct((2, 2, owned, RESIDUES, SUB, LANES), BF16),
            jax.ShapeDtypeStruct((2 * reach + 1, groups, owned, 2 * MAXLAG), F32),
        ),
        in_specs=[smem, smem] + [vmem] * 6,
        out_specs=(vmem, anywhere),
        scratch_shapes=lag_work(groups, owned),
        name="own_pairs",
        **params(2),
    )(place, pair_mask, *white, *other, twist, inverse)
    for step, sides in enumerate(moved):
        for side, far in zip((-1, 1), sides):
            offset = reach + side * (step + 1)
            out = pl.pallas_call(
                functools.partial(far_pairs_kernel, span, owned, offset, scale),
                out_shape=jax.ShapeDtypeStruct(out.shape, out.dtype),
                in_specs=[smem, smem] + [vmem] * (span + 5) + [anywhere],
                out_specs=anywhere,
                scratch_shapes=[VMEM((2, 2, groups, RESIDUES, SUB, LANES), BF16)]
                + spectra_work(groups)
                + lag_work(groups, owned),
                input_output_aliases={span + 7: 0},
                name="far_pairs",
                **params(4),
            )(place, pair_mask, *segments(far), own, twist, dft, band, inverse, out)
    return out


def solution(mesh):
    placed = (
        P(("fibre", "chan"), "win", "tm"),
        P(),
        P(("fibre", "win")),
        P(("fibre", "chan"), None),
    )
    return jax.shard_map(
        shards,
        mesh=mesh,
        in_specs=placed,
        out_specs=P(None, "win", ("fibre", "chan", "tm"), None),
        check_vma=False,
    )
```

```python
import functools
import math

import jax
import jax.numpy as jnp
import numpy as np
from jax import lax
from jax.experimental import pallas as pl
from jax.experimental.pallas import tpu as pltpu
from jax.sharding import PartitionSpec as P

MAXLAG = 1920
COST = (5000, 5000, 500, 500, 500)
BAND = 64
EPSILON = 1e-06

LANES = 128
ROWS = 32
RESIDUES = ROWS // 2 + 1
BLOCK = 4 * LANES
SUB = 8
F32 = jnp.float32
BF16 = jnp.bfloat16
VMEM = pltpu.VMEM


def halves(table):
    high = table.astype(np.float32).astype(jnp.bfloat16)
    low = (table - high.astype(np.float64)).astype(np.float32).astype(jnp.bfloat16)
    return np.stack([high, low])


def forward_table():
    angle = 2.0 * np.pi / LANES * (np.outer(np.arange(LANES), np.arange(LANES)) % LANES)
    cos, sin = np.cos(angle), np.sin(angle)
    return halves(np.block([[cos, -sin], [sin, cos]]))


def inverse_table():
    angle = 2.0 * np.pi / LANES * (np.outer(np.arange(LANES), np.arange(LANES)) % LANES)
    cos, sin = np.cos(angle), np.sin(angle)
    return halves(np.block([[cos, sin], [-sin, cos]]))


def twist_table():
    angle = 2.0 * np.pi / (ROWS * LANES) * np.outer(np.arange(RESIDUES), np.arange(LANES))
    both = np.stack([np.cos(angle), np.sin(angle)]).astype(np.float32)
    return np.ascontiguousarray(np.broadcast_to(both[:, :, None, :], (2, RESIDUES, SUB, LANES)))


def band_table():
    place = np.arange(LANES)
    place = np.minimum(place, LANES - 1 - place)
    band = place // (BAND // ROWS)
    return (band[:, None] == band[None, :]).astype(np.float32).astype(jnp.bfloat16)


def turn(value, k, n):
    real, imag = value
    c, s = math.cos(2 * math.pi * k / n), math.sin(2 * math.pi * k / n)
    if 8 * k == n:
        return ((real + imag) * c, (imag - real) * c)
    if 8 * k == 3 * n:
        return ((imag - real) * s, -(real + imag) * s)
    return (real * c + imag * s, imag * c - real * s)


def real_transform(x):
    n = len(x)
    if n == 2:
        return [(x[0] + x[1], None), (x[0] - x[1], None)]
    even, odd = real_transform(x[0::2]), real_transform(x[1::2])
    out = [None] * (n // 2 + 1)
    out[0] = (even[0][0] + odd[0][0], None)
    out[n // 2] = (even[0][0] - odd[0][0], None)
    for k in range(1, n // 4):
        er, ei = even[k]
        tr, ti = turn(odd[k], k, n)
        out[k] = (er + tr, ei + ti)
        out[n // 2 - k] = (er - tr, ti - ei)
    out[n // 4] = (even[n // 4][0], -odd[n // 4][0])
    return out


def real_inverse(x):
    n = 2 * (len(x) - 1)
    if n == 2:
        return [x[0][0] + x[1][0], x[0][0] - x[1][0]]
    even, odd = [None] * (n // 4 + 1), [None] * (n // 4 + 1)
    even[0] = (x[0][0] + x[n // 2][0], None)
    odd[0] = (x[0][0] - x[n // 2][0], None)
    for k in range(1, n // 4):
        ar, ai = x[k]
        br, bi = x[n // 2 - k]
        even[k] = (ar + br, ai - bi)
        dr, di = turn((ar - br, -(ai + bi)), k, n)
        odd[k] = (dr, -di)
    even[n // 4] = (2.0 * x[n // 4][0], None)
    odd[n // 4] = (-2.0 * x[n // 4][1], None)
    a, b = real_inverse(even), real_inverse(odd)
    return [v for pair in zip(a, b) for v in pair]


def split(value):
    high = value.astype(BF16)
    return high, (value - high.astype(F32)).astype(BF16)


def three_pass(high, low, table_ref):
    def dot(a, b):
        return jnp.dot(a, b, preferred_element_type=F32)

    return dot(high, table_ref[0]) + dot(low, table_ref[0]) + dot(high, table_ref[1])


def decimate_kernel(
    by, place_ref, end_hbm, taps_hbm, rec_hbm, keep_ref, send_ref, *refs
):
    rec_ref, lhs_ref, taps_ref, end_ref, rec_sem, small_sem = refs[-6:]
    whole_ref = refs[0] if len(refs) == 7 else None
    channels, windows, length = rec_ref.shape
    half = channels // 2
    rows = half * windows
    blocks = length // BLOCK
    pieces = rec_sem.shape[0]
    piece = length // pieces
    taps = taps_hbm.shape[1]
    small = [
        pltpu.make_async_copy(end_hbm, end_ref, small_sem.at[0]),
        pltpu.make_async_copy(taps_hbm, taps_ref, small_sem.at[1]),
    ]
    copies = [
        pltpu.make_async_copy(
            rec_hbm.at[:, :, k * piece : (k + 1) * piece],
            rec_ref.at[:, :, k * piece : (k + 1) * piece],
            rec_sem.at[k],
        )
        for k in range(pieces)
    ]
    for copy in small + copies:
        copy.start()
    row = lax.broadcasted_iota(jnp.int32, (windows, BLOCK), 0)
    lane = lax.broadcasted_iota(jnp.int32, (windows, BLOCK), 1)
    tap = lax.broadcasted_iota(jnp.int32, (taps, BLOCK + LANES), 0)
    at = lax.broadcasted_iota(jnp.int32, (taps, BLOCK + LANES), 1)
    chosen = jnp.where(tap + at == LANES + 3, 1.0, 0.0).astype(BF16)
    for copy in small:
        copy.wait()
    base = jnp.dot(
        jnp.broadcast_to(taps_ref[...].astype(F32), (SUB, taps)).astype(BF16), chosen,
        preferred_element_type=F32,
    )
    tap_table = pltpu.roll(
        jnp.broadcast_to(base[0:1], (LANES, BLOCK + LANES)), 0, 1, stride=4, stride_axis=0
    ).astype(BF16)
    end = jnp.zeros((windows, BLOCK), jnp.int32)
    for w in range(windows):
        end = jnp.where(row == w, end_ref[w], end)
    end = end - place_ref[0] * length - lane
    for h in range(2):
        lhs_ref[h, 0, :, 0:LANES] = jnp.zeros((rows, LANES), BF16)
        lhs_ref[h, blocks, :, LANES:] = jnp.zeros((rows, BLOCK), BF16)
    for b in range(blocks):
        if b * BLOCK % piece == 0:
            copies[b * BLOCK // piece].wait()
        for h in range(2):
            side = place_ref[by] if h == 0 else 1 - place_ref[by]
            x = rec_ref[pl.ds(side * half, half), :, b * BLOCK : (b + 1) * BLOCK].astype(F32)
            x = jnp.where((end > b * BLOCK)[None], x, 0.0)
            x = x.reshape(rows, BLOCK).astype(BF16)
            lhs_ref[h, b, :, LANES:] = x
            lhs_ref[h, b + 1, :, 0:LANES] = x[:, BLOCK - LANES :]
    for h, out_ref in ((0, keep_ref), (1, send_ref)):
        out = lax.dot_general(
            lhs_ref[h].reshape((blocks + 1) * rows, BLOCK + LANES),
            tap_table,
            (((1,), (1,)), ((), ())),
            preferred_element_type=F32,
        )
        out = out.reshape(blocks + 1, half, windows, LANES).astype(BF16)
        out_ref[...] = out
        if whole_ref is not None:
            whole_ref[place_ref[by] if h == 0 else 1 - place_ref[by]] = out


def decimate(records, filter_taps, segment_end, place, by, whole):
    channels, windows, length = records.shape
    blocks = length // BLOCK
    piece = jax.ShapeDtypeStruct((blocks + 1, channels // 2, windows, LANES), BF16)
    both = jax.ShapeDtypeStruct((2, *piece.shape), BF16)
    return pl.pallas_call(
        functools.partial(decimate_kernel, by),
        out_shape=(piece, piece, both) if whole else (piece, piece),
        in_specs=[pl.BlockSpec(memory_space=pltpu.SMEM)] + [pl.BlockSpec(memory_space=pltpu.HBM)] * 3,
        out_specs=(pl.BlockSpec(memory_space=VMEM),) * (3 if whole else 2),
        scratch_shapes=[
            VMEM(records.shape, BF16),
            VMEM((2, blocks + 1, channels // 2 * windows, BLOCK + LANES), BF16),
            VMEM((1, filter_taps.shape[0]), BF16),
            pltpu.SMEM(segment_end.shape, jnp.int32),
            pltpu.SemaphoreType.DMA((4,)),
            pltpu.SemaphoreType.DMA((2,)),
        ],
        compiler_params=pltpu.CompilerParams(vmem_limit_bytes=24 << 20),
        cost_estimate=pl.CostEstimate(
            flops=2 * records.size // 4 * BLOCK, bytes_accessed=3 * records.size, transcendentals=0
        ),
        name="decimate",
    )(place, *(pltpu.with_memory_space_constraint(a, pltpu.HBM) for a in (segment_end, filter_taps.reshape(1, -1), records)))


def join_kernel(first_ref, second_ref, out_ref):
    out_ref[0] = first_ref[...]
    out_ref[1] = second_ref[...]


def join(first, second):
    vmem = pl.BlockSpec(memory_space=VMEM)
    return pl.pallas_call(
        join_kernel,
        out_shape=jax.ShapeDtypeStruct((2, *first.shape), first.dtype),
        in_specs=[vmem, vmem],
        out_specs=vmem,
        name="join",
        **params(0.2),
    )(first, second)


def spectra(load, flags, tables, work, store):
    twist_ref, dft_ref, band_ref = tables
    high_ref, low_ref, spec_ref, power_ref = work
    groups, span = high_ref.shape[0], len(flags)
    depth = ROWS // span

    def first(g, carry):
        x = []
        for s in range(span):
            for r in range(depth):
                value = load(s, r, g).astype(F32)
                if r == 0:
                    value = value + load((s - 1) % span, depth, g).astype(F32) * flags[s]
                x.append(value)
        for q, (real, imag) in enumerate(real_transform(x)):
            if q == 0:
                turned = (real, jnp.zeros_like(real))
            else:
                cos, sin = twist_ref[0, q], twist_ref[1, q]
                if imag is None:
                    turned = (real * cos, -(real * sin))
                else:
                    turned = (real * cos + imag * sin, imag * cos - real * sin)
            for part in range(2):
                high, low = split(turned[part])
                high_ref[g, q, :, part * LANES : (part + 1) * LANES] = high
                low_ref[g, q, :, part * LANES : (part + 1) * LANES] = low
        return carry

    for g in range(groups):
        first(g, 0)
    count = groups * RESIDUES * SUB
    spec = three_pass(
        high_ref[...].reshape(count, 2 * LANES), low_ref[...].reshape(count, 2 * LANES), dft_ref
    )
    spec_ref[...] = spec.reshape(groups, RESIDUES, SUB, 2 * LANES)
    lower = (lax.broadcasted_iota(jnp.int32, (SUB, LANES), 1) < LANES // 2).astype(F32)

    def powers(g, carry):
        ends = inner = None
        for q in range(RESIDUES):
            real, imag = spec_ref[g, q, :, :LANES], spec_ref[g, q, :, LANES:]
            power = real * real + imag * imag
            if q in (0, RESIDUES - 1):
                ends = power if ends is None else ends + power
            else:
                inner = power if inner is None else inner + power
        power_ref[g] = inner + ends * lower
        return carry

    for g in range(groups):
        powers(g, 0)
    high, low = split(power_ref[...].reshape(groups * SUB, LANES))
    energy = jnp.dot(high, band_ref[...], preferred_element_type=F32) + jnp.dot(
        low, band_ref[...], preferred_element_type=F32
    )
    power_ref[...] = lax.rsqrt(energy * (1.0 / BAND) + EPSILON).reshape(groups, SUB, LANES)
    lane = lax.broadcasted_iota(jnp.int32, (SUB, LANES), 1)
    nonzero = (lane > 0).astype(F32)

    def whiten(g, carry):
        scale = power_ref[g]
        for q in range(RESIDUES):
            factor = scale
            if q == 0:
                factor = scale * lower * nonzero
            elif q == RESIDUES - 1:
                factor = scale * lower
            for part in range(2):
                value = spec_ref[g, q, :, part * LANES : (part + 1) * LANES]
                store(part, g, q, (value * factor).astype(BF16))
        return carry

    for g in range(groups):
        whiten(g, 0)


def gather_rows(values):
    row = lax.broadcasted_iota(jnp.int32, (SUB, LANES), 0)
    step = SUB // 2
    while step:
        lower = (row % (2 * step)) < step
        values = [
            jnp.where(lower, a, b) + pltpu.roll(jnp.where(lower, b, a), step, 0)
            if step == SUB // 2
            else jnp.where(lower, a, b) + swap(jnp.where(lower, b, a), step, lower)
            for a, b in zip(values[:step], values[step:])
        ]
        step //= 2
    return values[0]


def swap(value, step, lower):
    return jnp.where(lower, pltpu.roll(value, SUB - step, 0), pltpu.roll(value, step, 0))


def cross_rows(owned, js, windows, part_of_own, part_of_remote):
    groups = []
    loaded = [[[part_of_own(w, p, i).astype(F32) for p in range(2)] for i in range(owned)] for w in range(windows)]
    for first in range(0, js * owned, SUB):
        real, imag = [], []
        for pair in range(first, first + SUB):
            j, i = pair // owned, pair % owned
            re = im = None
            for w in range(windows):
                ar, ai = loaded[w][i]
                br, bi = (part_of_remote(w, p, j).astype(F32) for p in range(2))
                r = ar * br + ai * bi
                m = ai * br - ar * bi
                re = r if re is None else re + r
                im = m if im is None else im + m
            real.append(re)
            imag.append(im)
        groups.append((gather_rows(real), gather_rows(imag)))
    return groups


def lag_rows_of(sum_ref, group, twist_ref, weight):
    x = []
    for q in range(RESIDUES):
        real, imag = sum_ref[group, q, :, :LANES], sum_ref[group, q, :, LANES:]
        if q == 0:
            x.append((real, None))
            continue
        cos, sin = twist_ref[0, q], twist_ref[1, q]
        turned = real * cos - imag * sin
        if q == RESIDUES - 1:
            x.append((turned, None))
        else:
            x.append((0.5 * turned, 0.5 * (real * sin + imag * cos)))
    out = real_inverse(x)
    count = MAXLAG // LANES
    return [out[a] * weight for a in (*range(ROWS - count, ROWS), *range(count))]


def correlate(own_load, remote_load, chunks, owned, remotes, tables, work, weight, lag_ref):
    twist_ref, inverse_ref = tables
    high_ref, low_ref, sum_ref = work
    pair_groups = remotes * owned // SUB
    for q in range(RESIDUES):
        rows = cross_rows(
            owned, remotes, chunks,
            lambda w, p, i: own_load(w, p, i, q), lambda w, p, j: remote_load(w, p, j, q),
        )
        for group, parts in enumerate(rows):
            for part, value in enumerate(parts):
                high, low = split(value)
                high_ref[group, q, :, part * LANES : (part + 1) * LANES] = high
                low_ref[group, q, :, part * LANES : (part + 1) * LANES] = low
    count = pair_groups * RESIDUES * SUB
    total = three_pass(
        high_ref[...].reshape(count, 2 * LANES), low_ref[...].reshape(count, 2 * LANES), inverse_ref
    )
    sum_ref[...] = total.reshape(pair_groups, RESIDUES, SUB, 2 * LANES)
    per = SUB // owned
    for group in range(pair_groups):
        for place, value in enumerate(lag_rows_of(sum_ref, group, twist_ref, weight)):
            for j in range(per):
                lag_ref[group * per + j, :, place * LANES : (place + 1) * LANES] = value[
                    j * owned : (j + 1) * owned
                ]


def write_out(lag_ref, out_ref, offset, sem):
    copy = pltpu.make_async_copy(lag_ref, out_ref.at[offset], sem)
    copy.start()
    copy.wait()


def flags_of(place_ref, span):
    t = place_ref[0]
    return [((t + s) % span != 0).astype(F32) for s in range(span)]


def whiten_kernel(span, place_ref, *refs):
    pieces = refs[:span]
    twist_ref, dft_ref, band_ref = refs[span : span + 3]
    white_refs = refs[span + 3 : span + 5]
    work = refs[span + 5 :]
    flags = flags_of(place_ref, span)
    for c in range(2):

        def store(part, g, q, value, c=c):
            white_refs[c][part, g, q] = value

        def load(s, r, g, c=c):
            return pieces[s][c, r, g]

        spectra(load, flags, (twist_ref, dft_ref, band_ref), work, store)


def own_pairs_kernel(
    owned, offset, scale, place_ref, mask_ref, *refs,
):
    white_refs, other_refs = refs[:2], refs[2:4]
    twist_ref, inverse_ref, own_ref, out_ref, high_ref, low_ref, sum_ref, lag_ref, sem = refs[4:]
    groups = white_refs[0].shape[1]
    first = place_ref[0] * owned
    inside = lax.rem(first, groups)
    here = lax.div(first, groups) == place_ref[1]

    @pl.when(here)
    def _():
        for c in range(2):
            own_ref[c] = white_refs[c][:, pl.ds(inside, owned)]

    @pl.when(jnp.logical_not(here))
    def _():
        for c in range(2):
            own_ref[c] = other_refs[1 - c][:, pl.ds(inside, owned)]

    correlate(
        lambda c, p, i, q: own_ref[c, p, i, q],
        lambda c, p, j, q: white_refs[c][p, j, q],
        2, owned, groups, (twist_ref, inverse_ref), (high_ref, low_ref, sum_ref),
        mask_ref[0, offset].astype(F32) * scale, lag_ref,
    )
    write_out(lag_ref, out_ref, offset, sem)


def far_pairs_kernel(span, owned, offset, scale, place_ref, mask_ref, *refs):
    pieces = refs[:span]
    own_ref, twist_ref, dft_ref, band_ref, inverse_ref, _, out_ref = refs[span : span + 7]
    (
        white_ref, zhigh_ref, zlow_ref, spec_ref, power_ref, high_ref, low_ref, sum_ref, lag_ref, sem,
    ) = refs[span + 7 :]
    flags = flags_of(place_ref, span)
    groups = white_ref.shape[2]
    for c in range(2):

        def store(part, g, q, value, c=c):
            white_ref[c, part, g, q] = value

        def load(s, r, g, c=c):
            return pieces[s][c, r, g]

        spectra(
            load, flags, (twist_ref, dft_ref, band_ref),
            (zhigh_ref, zlow_ref, spec_ref, power_ref), store,
        )
    correlate(
        lambda c, p, i, q: own_ref[c, p, i, q],
        lambda c, p, j, q: white_ref[c, p, j, q],
        2, owned, groups, (twist_ref, inverse_ref), (high_ref, low_ref, sum_ref),
        mask_ref[0, offset].astype(F32) * scale, lag_ref,
    )
    write_out(lag_ref, out_ref, offset, sem)


def own_spectra_kernel(place_ref, mine_ref, theirs_ref, twist_ref, dft_ref, band_ref, away_ref, here_ref, *work):
    flags = flags_of(place_ref, 2)
    for side, white_ref in ((1 - place_ref[1], away_ref), (place_ref[1], here_ref)):

        def load(s, r, g, side=side):
            return (mine_ref, theirs_ref)[s][side, r, g]

        def store(part, g, q, value, white_ref=white_ref):
            white_ref[part, g, q] = value

        spectra(load, flags, (twist_ref, dft_ref, band_ref), work, store)


def far_spectra_kernel(place_ref, mine_ref, relayed_ref, twist_ref, dft_ref, band_ref, white_ref, *work):
    def load(s, r, g):
        return (mine_ref, relayed_ref)[s][r, g]

    def store(part, g, q, value):
        white_ref[part, g, q] = value

    spectra(load, flags_of(place_ref, 2), (twist_ref, dft_ref, band_ref), work, store)


def far_cross_kernel(mine_ref, theirs_ref, far_ref, fars_ref, across_ref, back_ref):
    own, far = (mine_ref, theirs_ref), (far_ref, fars_ref)
    for q in range(RESIDUES):
        rows = cross_rows(4, 4, 2, lambda w, p, i: own[w][p, i, q], lambda w, p, j: far[w][p, j, q])
        for group, parts in enumerate(rows):
            for part, value in enumerate(parts):
                at = slice(part * LANES, (part + 1) * LANES)
                value = value.astype(BF16)
                across_ref[group, q, :, at] = value
                back_ref[group, q, :, at] = value if part == 0 else -value


def near_pairs_kernel(
    offset, scale, place_ref, mask_ref, away_ref, here_ref, others_here_ref, others_away_ref,
    twist_ref, inverse_ref, out_ref, own_ref, high_ref, low_ref, sum_ref, lag_ref, sem,
):
    same = place_ref[0] == place_ref[1]

    @pl.when(same)
    def _():
        own_ref[0] = here_ref[...]
        own_ref[1] = others_away_ref[...]

    @pl.when(jnp.logical_not(same))
    def _():
        own_ref[0] = away_ref[...]
        own_ref[1] = others_here_ref[...]

    half = (here_ref, others_away_ref)
    correlate(
        lambda w, p, i, q: own_ref[w, p, i, q],
        lambda w, p, j, q: half[w][p, j, q],
        2, 4, 4, (twist_ref, inverse_ref), (high_ref, low_ref, sum_ref),
        mask_ref[0, offset].astype(F32) * scale, lag_ref,
    )
    write_out(lag_ref, out_ref, offset, sem)


def lags_kernel(offset, scale, mirrored, mask_ref, cross_ref, twist_ref, inverse_ref, _, out_ref, sum_ref, lag_ref, sem):
    rows = cross_ref[...].reshape(2 * RESIDUES * SUB, 2 * LANES)
    total = jnp.dot(rows, inverse_ref[0], preferred_element_type=F32) + jnp.dot(
        rows, inverse_ref[1], preferred_element_type=F32
    )
    sum_ref[...] = total.reshape(2, RESIDUES, SUB, 2 * LANES)
    weight = mask_ref[0, offset].astype(F32) * scale
    for group in range(2):
        for place, value in enumerate(lag_rows_of(sum_ref, group, twist_ref, weight)):
            at = slice(place * LANES, (place + 1) * LANES)
            if mirrored:
                for row in range(SUB):
                    lag_ref[row % 4, group * 2 + row // 4, at] = value[row]
            else:
                for j in range(2):
                    lag_ref[group * 2 + j, :, at] = value[4 * j : 4 * j + 4]
    write_out(lag_ref, out_ref, offset, sem)


def mirrored(records, filter_taps, segment_end, pair_mask, place, tables, scale):
    twist, dft, inverse, band = tables
    smem, vmem = pl.BlockSpec(memory_space=pltpu.SMEM), pl.BlockSpec(memory_space=VMEM)
    anywhere = pl.BlockSpec(memory_space=pl.ANY)
    blocks = lax.axis_size("chan")
    white = jax.ShapeDtypeStruct((2, 4, RESIDUES, SUB, LANES), BF16)
    spec = jax.ShapeDtypeStruct((2, RESIDUES, SUB, 2 * LANES), BF16)
    shape = jax.ShapeDtypeStruct((3, 4, 4, 2 * MAXLAG), F32)

    def exchange(array, axis):
        return lax.ppermute(array, axis, [(0, 1), (1, 0)])

    def along(array, by):
        return lax.ppermute(array, "chan", [(i, (i + by) % blocks) for i in range(blocks)])

    def across(array):
        pairs = [(0, 0), (1, 2), (2, 1), (3, 3)]
        return lax.ppermute(array, ("tm", "win"), pairs)

    keep, send, both = decimate(records, filter_taps, segment_end, place, 0, True)
    far_send, far_keep = along(send, 1), along(keep, 1)
    theirs = exchange(both, "tm")
    relayed = exchange(far_send, "tm")
    away, here = pl.pallas_call(
        own_spectra_kernel,
        out_shape=(white, white),
        in_specs=[smem] + [vmem] * 5,
        out_specs=(vmem, vmem),
        scratch_shapes=spectra_work(4),
        name="own_spectra",
        **params(COST[0]),
    )(place, both, theirs, twist, dft, band)
    (away, here), relayed = lax.optimization_barrier(((away, here), relayed))
    others_away, others_here = exchange(away, "win"), exchange(here, "win")
    far = pl.pallas_call(
        far_spectra_kernel,
        out_shape=white,
        in_specs=[smem] + [vmem] * 5,
        out_specs=vmem,
        scratch_shapes=spectra_work(4),
        name="far_spectra",
        **params(COST[1]),
    )(place, far_keep, relayed, twist, dft, band)
    fars = exchange(far, "win")
    crossed, back = pl.pallas_call(
        far_cross_kernel,
        out_shape=(spec, spec),
        in_specs=[vmem] * 4,
        out_specs=(vmem, vmem),
        name="far_cross",
        **params(COST[2]),
    )(here, others_away, far, fars)
    crossed, back = across(crossed), along(back, -1)
    out = pl.pallas_call(
        functools.partial(near_pairs_kernel, 1, scale),
        out_shape=shape,
        in_specs=[smem, smem] + [vmem] * 6,
        out_specs=anywhere,
        scratch_shapes=[VMEM((2, 2, 4, RESIDUES, SUB, LANES), BF16)] + lag_work(4, 4),
        name="near_pairs",
        **params(COST[3]),
    )(place, pair_mask, away, here, others_here, others_away, twist, inverse)
    for offset, cross in ((0, crossed), (2, back)):
        out = pl.pallas_call(
            functools.partial(lags_kernel, offset, scale, offset == 2),
            out_shape=shape,
            in_specs=[smem] + [vmem] * 3 + [anywhere],
            out_specs=anywhere,
            scratch_shapes=lag_work(4, 4)[2:],
            input_output_aliases={4: 0},
            name="lags",
            **params(COST[4]),
        )(pair_mask, cross, twist, inverse, out)
    return out


def spectra_work(groups):
    return [
        VMEM((groups, RESIDUES, SUB, 2 * LANES), BF16),
        VMEM((groups, RESIDUES, SUB, 2 * LANES), BF16),
        VMEM((groups, RESIDUES, SUB, 2 * LANES), F32),
        VMEM((groups, SUB, LANES), F32),
    ]


def lag_work(groups, owned):
    pair_groups = groups * owned // SUB
    return [
        VMEM((pair_groups, RESIDUES, SUB, 2 * LANES), BF16),
        VMEM((pair_groups, RESIDUES, SUB, 2 * LANES), BF16),
        VMEM((pair_groups, RESIDUES, SUB, 2 * LANES), F32),
        VMEM((groups, owned, 2 * MAXLAG), F32),
        pltpu.SemaphoreType.DMA,
    ]


def params(microseconds):
    return dict(
        compiler_params=pltpu.CompilerParams(vmem_limit_bytes=16 << 20),
        cost_estimate=pl.CostEstimate(
            flops=int(microseconds * 1e6), bytes_accessed=1 << 10, transcendentals=0
        ),
    )


def shards(records, filter_taps, segment_end, pair_mask):
    span = lax.axis_size("tm")
    owned = records.shape[0] // span
    groups = records.shape[0] // 2
    reach = (pair_mask.shape[1] - 1) // 2
    windows = 2 * records.shape[1]
    scale = 1.0 / math.sqrt(windows * ROWS * LANES // 2)
    place = jnp.stack([lax.axis_index("tm"), lax.axis_index("win")]).astype(jnp.int32)
    twist, dft, inverse, band = (
        jnp.asarray(t) for t in (twist_table(), forward_table(), inverse_table(), band_table())
    )
    smem, vmem = pl.BlockSpec(memory_space=pltpu.SMEM), pl.BlockSpec(memory_space=VMEM)
    anywhere = pl.BlockSpec(memory_space=pl.ANY)

    def permute(array, axis, by):
        count = lax.axis_size(axis)
        return lax.ppermute(array, axis, [(i, (i + by) % count) for i in range(count)])

    def segments(chunk):
        return [chunk] + [permute(chunk, "tm", -s) for s in range(1, span)]

    if span == 2 and reach == 1 and groups == 4:
        return mirrored(records, filter_taps, segment_end, pair_mask, place, (twist, dft, inverse, band), scale)
    keep, send = decimate(records, filter_taps, segment_end, place, 1, False)
    received = permute(send, "win", 1)
    block = join(keep, received)
    up = down = block
    moved = []
    for _ in range(reach):
        up, down = permute(up, "chan", 1), permute(down, "chan", -1)
        moved.append([up, down])
    mine = segments(block)
    white = pl.pallas_call(
        functools.partial(whiten_kernel, span),
        out_shape=(jax.ShapeDtypeStruct((2, groups, RESIDUES, SUB, LANES), BF16),) * 2,
        in_specs=[smem] + [vmem] * (span + 3),
        out_specs=(vmem,) * 2,
        scratch_shapes=spectra_work(groups),
        name="whiten",
        **params(3),
    )(place, *mine, twist, dft, band)
    other = [permute(part, "win", 1) for part in white]
    own, out = pl.pallas_call(
        functools.partial(own_pairs_kernel, owned, reach, scale),
        out_shape=(
            jax.ShapeDtypeStruct((2, 2, owned, RESIDUES, SUB, LANES), BF16),
            jax.ShapeDtypeStruct((2 * reach + 1, groups, owned, 2 * MAXLAG), F32),
        ),
        in_specs=[smem, smem] + [vmem] * 6,
        out_specs=(vmem, anywhere),
        scratch_shapes=lag_work(groups, owned),
        name="own_pairs",
        **params(2),
    )(place, pair_mask, *white, *other, twist, inverse)
    for step, sides in enumerate(moved):
        for side, far in zip((-1, 1), sides):
            offset = reach + side * (step + 1)
            out = pl.pallas_call(
                functools.partial(far_pairs_kernel, span, owned, offset, scale),
                out_shape=jax.ShapeDtypeStruct(out.shape, out.dtype),
                in_specs=[smem, smem] + [vmem] * (span + 5) + [anywhere],
                out_specs=anywhere,
                scratch_shapes=[VMEM((2, 2, groups, RESIDUES, SUB, LANES), BF16)]
                + spectra_work(groups)
                + lag_work(groups, owned),
                input_output_aliases={span + 7: 0},
                name="far_pairs",
                **params(4),
            )(place, pair_mask, *segments(far), own, twist, dft, band, inverse, out)
    return out


def solution(mesh):
    placed = (
        P(("fibre", "chan"), "win", "tm"),
        P(),
        P(("fibre", "win")),
        P(("fibre", "chan"), None),
    )
    return jax.shard_map(
        shards,
        mesh=mesh,
        in_specs=placed,
        out_specs=P(None, "win", ("fibre", "chan", "tm"), None),
        check_vma=False,
    )
```

```python
import functools
import math

import jax
import jax.numpy as jnp
import numpy as np
from jax import lax
from jax.experimental import pallas as pl
from jax.experimental.pallas import tpu as pltpu
from jax.sharding import PartitionSpec as P

MAXLAG = 1920
COST = (5000, 5000, 500, 500, 500)
BAND = 64
EPSILON = 1e-06

LANES = 128
ROWS = 32
RESIDUES = ROWS // 2 + 1
BLOCK = 4 * LANES
SUB = 8
F32 = jnp.float32
BF16 = jnp.bfloat16
VMEM = pltpu.VMEM


def halves(table):
    high = table.astype(np.float32).astype(jnp.bfloat16)
    low = (table - high.astype(np.float64)).astype(np.float32).astype(jnp.bfloat16)
    return np.stack([high, low])


def forward_table():
    angle = 2.0 * np.pi / LANES * (np.outer(np.arange(LANES), np.arange(LANES)) % LANES)
    cos, sin = np.cos(angle), np.sin(angle)
    return halves(np.block([[cos, -sin], [sin, cos]]))


def inverse_table():
    angle = 2.0 * np.pi / LANES * (np.outer(np.arange(LANES), np.arange(LANES)) % LANES)
    cos, sin = np.cos(angle), np.sin(angle)
    return halves(np.block([[cos, sin], [-sin, cos]]))


def twist_table():
    angle = 2.0 * np.pi / (ROWS * LANES) * np.outer(np.arange(RESIDUES), np.arange(LANES))
    both = np.stack([np.cos(angle), np.sin(angle)]).astype(np.float32)
    return np.ascontiguousarray(np.broadcast_to(both[:, :, None, :], (2, RESIDUES, SUB, LANES)))


def band_table():
    place = np.arange(LANES)
    place = np.minimum(place, LANES - 1 - place)
    band = place // (BAND // ROWS)
    return (band[:, None] == band[None, :]).astype(np.float32).astype(jnp.bfloat16)


def turn(value, k, n):
    real, imag = value
    c, s = math.cos(2 * math.pi * k / n), math.sin(2 * math.pi * k / n)
    if 8 * k == n:
        return ((real + imag) * c, (imag - real) * c)
    if 8 * k == 3 * n:
        return ((imag - real) * s, -(real + imag) * s)
    return (real * c + imag * s, imag * c - real * s)


def real_transform(x):
    n = len(x)
    if n == 2:
        return [(x[0] + x[1], None), (x[0] - x[1], None)]
    even, odd = real_transform(x[0::2]), real_transform(x[1::2])
    out = [None] * (n // 2 + 1)
    out[0] = (even[0][0] + odd[0][0], None)
    out[n // 2] = (even[0][0] - odd[0][0], None)
    for k in range(1, n // 4):
        er, ei = even[k]
        tr, ti = turn(odd[k], k, n)
        out[k] = (er + tr, ei + ti)
        out[n // 2 - k] = (er - tr, ti - ei)
    out[n // 4] = (even[n // 4][0], -odd[n // 4][0])
    return out


def real_inverse(x):
    n = 2 * (len(x) - 1)
    if n == 2:
        return [x[0][0] + x[1][0], x[0][0] - x[1][0]]
    even, odd = [None] * (n // 4 + 1), [None] * (n // 4 + 1)
    even[0] = (x[0][0] + x[n // 2][0], None)
    odd[0] = (x[0][0] - x[n // 2][0], None)
    for k in range(1, n // 4):
        ar, ai = x[k]
        br, bi = x[n // 2 - k]
        even[k] = (ar + br, ai - bi)
        dr, di = turn((ar - br, -(ai + bi)), k, n)
        odd[k] = (dr, -di)
    even[n // 4] = (2.0 * x[n // 4][0], None)
    odd[n // 4] = (-2.0 * x[n // 4][1], None)
    a, b = real_inverse(even), real_inverse(odd)
    return [v for pair in zip(a, b) for v in pair]


def split(value):
    high = value.astype(BF16)
    return high, (value - high.astype(F32)).astype(BF16)


def three_pass(high, low, table_ref):
    def dot(a, b):
        return jnp.dot(a, b, preferred_element_type=F32)

    return dot(high, table_ref[0]) + dot(low, table_ref[0]) + dot(high, table_ref[1])


def decimate_kernel(
    by, place_ref, end_hbm, taps_hbm, rec_hbm, keep_ref, send_ref,
    rec_ref, lhs_ref, taps_ref, end_ref, rec_sem, small_sem,
):
    channels, windows, length = rec_ref.shape
    half = channels // 2
    rows = half * windows
    blocks = length // BLOCK
    pieces = rec_sem.shape[0]
    piece = length // pieces
    taps = taps_hbm.shape[1]
    small = [
        pltpu.make_async_copy(end_hbm, end_ref, small_sem.at[0]),
        pltpu.make_async_copy(taps_hbm, taps_ref, small_sem.at[1]),
    ]
    copies = [
        pltpu.make_async_copy(
            rec_hbm.at[:, :, k * piece : (k + 1) * piece],
            rec_ref.at[:, :, k * piece : (k + 1) * piece],
            rec_sem.at[k],
        )
        for k in range(pieces)
    ]
    for copy in small + copies:
        copy.start()
    row = lax.broadcasted_iota(jnp.int32, (windows, BLOCK), 0)
    lane = lax.broadcasted_iota(jnp.int32, (windows, BLOCK), 1)
    tap = lax.broadcasted_iota(jnp.int32, (taps, BLOCK + LANES), 0)
    at = lax.broadcasted_iota(jnp.int32, (taps, BLOCK + LANES), 1)
    chosen = jnp.where(tap + at == LANES + 3, 1.0, 0.0).astype(BF16)
    for copy in small:
        copy.wait()
    base = jnp.dot(
        jnp.broadcast_to(taps_ref[...].astype(F32), (SUB, taps)).astype(BF16), chosen,
        preferred_element_type=F32,
    )
    tap_table = pltpu.roll(
        jnp.broadcast_to(base[0:1], (LANES, BLOCK + LANES)), 0, 1, stride=4, stride_axis=0
    ).astype(BF16)
    end = jnp.zeros((windows, BLOCK), jnp.int32)
    for w in range(windows):
        end = jnp.where(row == w, end_ref[w], end)
    end = end - place_ref[0] * length - lane
    for h in range(2):
        lhs_ref[h, 0, :, 0:LANES] = jnp.zeros((rows, LANES), BF16)
        lhs_ref[h, blocks, :, LANES:] = jnp.zeros((rows, BLOCK), BF16)
    for b in range(blocks):
        if b * BLOCK % piece == 0:
            copies[b * BLOCK // piece].wait()
        for h in range(2):
            side = place_ref[by] if h == 0 else 1 - place_ref[by]
            x = rec_ref[pl.ds(side * half, half), :, b * BLOCK : (b + 1) * BLOCK].astype(F32)
            x = jnp.where((end > b * BLOCK)[None], x, 0.0)
            x = x.reshape(rows, BLOCK).astype(BF16)
            lhs_ref[h, b, :, LANES:] = x
            lhs_ref[h, b + 1, :, 0:LANES] = x[:, BLOCK - LANES :]
    for h, out_ref in ((0, keep_ref), (1, send_ref)):
        out = lax.dot_general(
            lhs_ref[h].reshape((blocks + 1) * rows, BLOCK + LANES),
            tap_table,
            (((1,), (1,)), ((), ())),
            preferred_element_type=F32,
        )
        out_ref[...] = out.reshape(blocks + 1, half, windows, LANES).astype(BF16)


def decimate(records, filter_taps, segment_end, place, by):
    channels, windows, length = records.shape
    blocks = length // BLOCK
    piece = jax.ShapeDtypeStruct((blocks + 1, channels // 2, windows, LANES), BF16)
    return pl.pallas_call(
        functools.partial(decimate_kernel, by),
        out_shape=(piece, piece),
        in_specs=[pl.BlockSpec(memory_space=pltpu.SMEM)] + [pl.BlockSpec(memory_space=pltpu.HBM)] * 3,
        out_specs=(pl.BlockSpec(memory_space=VMEM),) * 2,
        scratch_shapes=[
            VMEM(records.shape, BF16),
            VMEM((2, blocks + 1, channels // 2 * windows, BLOCK + LANES), BF16),
            VMEM((1, filter_taps.shape[0]), BF16),
            pltpu.SMEM(segment_end.shape, jnp.int32),
            pltpu.SemaphoreType.DMA((4,)),
            pltpu.SemaphoreType.DMA((2,)),
        ],
        compiler_params=pltpu.CompilerParams(vmem_limit_bytes=24 << 20),
        cost_estimate=pl.CostEstimate(
            flops=2 * records.size // 4 * BLOCK, bytes_accessed=3 * records.size, transcendentals=0
        ),
        name="decimate",
    )(place, *(pltpu.with_memory_space_constraint(a, pltpu.HBM) for a in (segment_end, filter_taps.reshape(1, -1), records)))


def join_kernel(first_ref, second_ref, out_ref):
    out_ref[0] = first_ref[...]
    out_ref[1] = second_ref[...]


def join(first, second):
    vmem = pl.BlockSpec(memory_space=VMEM)
    return pl.pallas_call(
        join_kernel,
        out_shape=jax.ShapeDtypeStruct((2, *first.shape), first.dtype),
        in_specs=[vmem, vmem],
        out_specs=vmem,
        name="join",
        **params(0.2),
    )(first, second)


def spectra(load, flags, tables, work, store):
    twist_ref, dft_ref, band_ref = tables
    high_ref, low_ref, spec_ref, power_ref = work
    groups, span = high_ref.shape[0], len(flags)
    depth = ROWS // span

    def first(g, carry):
        x = []
        for s in range(span):
            for r in range(depth):
                value = load(s, r, g).astype(F32)
                if r == 0:
                    value = value + load((s - 1) % span, depth, g).astype(F32) * flags[s]
                x.append(value)
        for q, (real, imag) in enumerate(real_transform(x)):
            if q == 0:
                turned = (real, jnp.zeros_like(real))
            else:
                cos, sin = twist_ref[0, q], twist_ref[1, q]
                if imag is None:
                    turned = (real * cos, -(real * sin))
                else:
                    turned = (real * cos + imag * sin, imag * cos - real * sin)
            for part in range(2):
                high, low = split(turned[part])
                high_ref[g, q, :, part * LANES : (part + 1) * LANES] = high
                low_ref[g, q, :, part * LANES : (part + 1) * LANES] = low
        return carry

    for g in range(groups):
        first(g, 0)
    count = groups * RESIDUES * SUB
    spec = three_pass(
        high_ref[...].reshape(count, 2 * LANES), low_ref[...].reshape(count, 2 * LANES), dft_ref
    )
    spec_ref[...] = spec.reshape(groups, RESIDUES, SUB, 2 * LANES)
    lower = (lax.broadcasted_iota(jnp.int32, (SUB, LANES), 1) < LANES // 2).astype(F32)

    def powers(g, carry):
        ends = inner = None
        for q in range(RESIDUES):
            real, imag = spec_ref[g, q, :, :LANES], spec_ref[g, q, :, LANES:]
            power = real * real + imag * imag
            if q in (0, RESIDUES - 1):
                ends = power if ends is None else ends + power
            else:
                inner = power if inner is None else inner + power
        power_ref[g] = inner + ends * lower
        return carry

    for g in range(groups):
        powers(g, 0)
    high, low = split(power_ref[...].reshape(groups * SUB, LANES))
    energy = jnp.dot(high, band_ref[...], preferred_element_type=F32) + jnp.dot(
        low, band_ref[...], preferred_element_type=F32
    )
    power_ref[...] = lax.rsqrt(energy * (1.0 / BAND) + EPSILON).reshape(groups, SUB, LANES)
    lane = lax.broadcasted_iota(jnp.int32, (SUB, LANES), 1)
    nonzero = (lane > 0).astype(F32)

    def whiten(g, carry):
        scale = power_ref[g]
        for q in range(RESIDUES):
            factor = scale
            if q == 0:
                factor = scale * lower * nonzero
            elif q == RESIDUES - 1:
                factor = scale * lower
            for part in range(2):
                value = spec_ref[g, q, :, part * LANES : (part + 1) * LANES]
                store(part, g, q, (value * factor).astype(BF16))
        return carry

    for g in range(groups):
        whiten(g, 0)


def gather_rows(values):
    row = lax.broadcasted_iota(jnp.int32, (SUB, LANES), 0)
    step = SUB // 2
    while step:
        lower = (row % (2 * step)) < step
        values = [
            jnp.where(lower, a, b) + pltpu.roll(jnp.where(lower, b, a), step, 0)
            if step == SUB // 2
            else jnp.where(lower, a, b) + swap(jnp.where(lower, b, a), step, lower)
            for a, b in zip(values[:step], values[step:])
        ]
        step //= 2
    return values[0]


def swap(value, step, lower):
    return jnp.where(lower, pltpu.roll(value, SUB - step, 0), pltpu.roll(value, step, 0))


def cross_rows(owned, js, windows, part_of_own, part_of_remote):
    groups = []
    loaded = [[[part_of_own(w, p, i).astype(F32) for p in range(2)] for i in range(owned)] for w in range(windows)]
    for first in range(0, js * owned, SUB):
        real, imag = [], []
        for pair in range(first, first + SUB):
            j, i = pair // owned, pair % owned
            re = im = None
            for w in range(windows):
                ar, ai = loaded[w][i]
                br, bi = (part_of_remote(w, p, j).astype(F32) for p in range(2))
                r = ar * br + ai * bi
                m = ai * br - ar * bi
                re = r if re is None else re + r
                im = m if im is None else im + m
            real.append(re)
            imag.append(im)
        groups.append((gather_rows(real), gather_rows(imag)))
    return groups


def lag_rows_of(sum_ref, group, twist_ref, weight):
    x = []
    for q in range(RESIDUES):
        real, imag = sum_ref[group, q, :, :LANES], sum_ref[group, q, :, LANES:]
        if q == 0:
            x.append((real, None))
            continue
        cos, sin = twist_ref[0, q], twist_ref[1, q]
        turned = real * cos - imag * sin
        if q == RESIDUES - 1:
            x.append((turned, None))
        else:
            x.append((0.5 * turned, 0.5 * (real * sin + imag * cos)))
    out = real_inverse(x)
    count = MAXLAG // LANES
    return [out[a] * weight for a in (*range(ROWS - count, ROWS), *range(count))]


def correlate(own_load, remote_load, chunks, owned, remotes, tables, work, weight, lag_ref):
    twist_ref, inverse_ref = tables
    high_ref, low_ref, sum_ref = work
    pair_groups = remotes * owned // SUB
    for q in range(RESIDUES):
        rows = cross_rows(
            owned, remotes, chunks,
            lambda w, p, i: own_load(w, p, i, q), lambda w, p, j: remote_load(w, p, j, q),
        )
        for group, parts in enumerate(rows):
            for part, value in enumerate(parts):
                high, low = split(value)
                high_ref[group, q, :, part * LANES : (part + 1) * LANES] = high
                low_ref[group, q, :, part * LANES : (part + 1) * LANES] = low
    count = pair_groups * RESIDUES * SUB
    total = three_pass(
        high_ref[...].reshape(count, 2 * LANES), low_ref[...].reshape(count, 2 * LANES), inverse_ref
    )
    sum_ref[...] = total.reshape(pair_groups, RESIDUES, SUB, 2 * LANES)
    per = SUB // owned
    for group in range(pair_groups):
        for place, value in enumerate(lag_rows_of(sum_ref, group, twist_ref, weight)):
            for j in range(per):
                lag_ref[group * per + j, :, place * LANES : (place + 1) * LANES] = value[
                    j * owned : (j + 1) * owned
                ]


def write_out(lag_ref, out_ref, offset, sem):
    copy = pltpu.make_async_copy(lag_ref, out_ref.at[offset], sem)
    copy.start()
    copy.wait()


def flags_of(place_ref, span):
    t = place_ref[0]
    return [((t + s) % span != 0).astype(F32) for s in range(span)]


def whiten_kernel(span, place_ref, *refs):
    pieces = refs[:span]
    twist_ref, dft_ref, band_ref = refs[span : span + 3]
    white_refs = refs[span + 3 : span + 5]
    work = refs[span + 5 :]
    flags = flags_of(place_ref, span)
    for c in range(2):

        def store(part, g, q, value, c=c):
            white_refs[c][part, g, q] = value

        def load(s, r, g, c=c):
            return pieces[s][c, r, g]

        spectra(load, flags, (twist_ref, dft_ref, band_ref), work, store)


def own_pairs_kernel(
    owned, offset, scale, place_ref, mask_ref, *refs,
):
    white_refs, other_refs = refs[:2], refs[2:4]
    twist_ref, inverse_ref, own_ref, out_ref, high_ref, low_ref, sum_ref, lag_ref, sem = refs[4:]
    groups = white_refs[0].shape[1]
    first = place_ref[0] * owned
    inside = lax.rem(first, groups)
    here = lax.div(first, groups) == place_ref[1]

    @pl.when(here)
    def _():
        for c in range(2):
            own_ref[c] = white_refs[c][:, pl.ds(inside, owned)]

    @pl.when(jnp.logical_not(here))
    def _():
        for c in range(2):
            own_ref[c] = other_refs[1 - c][:, pl.ds(inside, owned)]

    correlate(
        lambda c, p, i, q: own_ref[c, p, i, q],
        lambda c, p, j, q: white_refs[c][p, j, q],
        2, owned, groups, (twist_ref, inverse_ref), (high_ref, low_ref, sum_ref),
        mask_ref[0, offset].astype(F32) * scale, lag_ref,
    )
    write_out(lag_ref, out_ref, offset, sem)


def far_pairs_kernel(span, owned, offset, scale, place_ref, mask_ref, *refs):
    pieces = refs[:span]
    own_ref, twist_ref, dft_ref, band_ref, inverse_ref, _, out_ref = refs[span : span + 7]
    (
        white_ref, zhigh_ref, zlow_ref, spec_ref, power_ref, high_ref, low_ref, sum_ref, lag_ref, sem,
    ) = refs[span + 7 :]
    flags = flags_of(place_ref, span)
    groups = white_ref.shape[2]
    for c in range(2):

        def store(part, g, q, value, c=c):
            white_ref[c, part, g, q] = value

        def load(s, r, g, c=c):
            return pieces[s][c, r, g]

        spectra(
            load, flags, (twist_ref, dft_ref, band_ref),
            (zhigh_ref, zlow_ref, spec_ref, power_ref), store,
        )
    correlate(
        lambda c, p, i, q: own_ref[c, p, i, q],
        lambda c, p, j, q: white_ref[c, p, j, q],
        2, owned, groups, (twist_ref, inverse_ref), (high_ref, low_ref, sum_ref),
        mask_ref[0, offset].astype(F32) * scale, lag_ref,
    )
    write_out(lag_ref, out_ref, offset, sem)


def own_spectra_kernel(
    place_ref, keep_ref, send_ref, their_keep_ref, their_send_ref, twist_ref, dft_ref, band_ref, white_ref, *work
):
    flags = flags_of(place_ref, 2)
    for at, side in enumerate((1 - place_ref[1], place_ref[1])):
        kept = side == place_ref[0]

        def load(s, r, g, kept=kept):
            if s == 0:
                return jnp.where(kept, keep_ref[r, g], send_ref[r, g])
            return jnp.where(kept, their_send_ref[r, g], their_keep_ref[r, g])

        def store(part, g, q, value, at=at):
            white_ref[at, part, g, q] = value

        spectra(load, flags, (twist_ref, dft_ref, band_ref), work, store)


def far_spectra_kernel(place_ref, mine_ref, relayed_ref, twist_ref, dft_ref, band_ref, white_ref, *work):
    def load(s, r, g):
        return (mine_ref, relayed_ref)[s][r, g]

    def store(part, g, q, value):
        white_ref[part, g, q] = value

    spectra(load, flags_of(place_ref, 2), (twist_ref, dft_ref, band_ref), work, store)


def far_cross_kernel(white_ref, others_ref, far_ref, fars_ref, back_ref):
    own, far = (white_ref.at[1], others_ref.at[0]), (far_ref, fars_ref)
    for q in range(RESIDUES):
        rows = cross_rows(4, 4, 2, lambda w, p, j: far[w][p, j, q], lambda w, p, i: own[w][p, i, q])
        for group, parts in enumerate(rows):
            for part, value in enumerate(parts):
                at = slice(part * LANES, (part + 1) * LANES)
                back_ref[group, q, :, at] = value.astype(BF16)


def near_pairs_kernel(
    offset, scale, place_ref, mask_ref, white_ref, others_ref,
    twist_ref, inverse_ref, lag_ref, own_ref, high_ref, low_ref, sum_ref,
):
    same = place_ref[0] == place_ref[1]

    @pl.when(same)
    def _():
        own_ref[0] = white_ref[1]
        own_ref[1] = others_ref[0]

    @pl.when(jnp.logical_not(same))
    def _():
        own_ref[0] = white_ref[0]
        own_ref[1] = others_ref[1]

    half = (white_ref.at[1], others_ref.at[0])
    correlate(
        lambda w, p, i, q: own_ref[w, p, i, q],
        lambda w, p, j, q: half[w][p, j, q],
        2, 4, 4, (twist_ref, inverse_ref), (high_ref, low_ref, sum_ref),
        mask_ref[0, offset].astype(F32) * scale, lag_ref,
    )


def lag_sums(cross_ref, inverse_ref, sum_ref, conjugate=False):
    rows = cross_ref[...].reshape(2 * RESIDUES * SUB, 2 * LANES)
    if conjugate:
        rows = jnp.concatenate([rows[:, :LANES], -rows[:, LANES:]], axis=1)
    total = jnp.dot(rows, inverse_ref[0], preferred_element_type=F32) + jnp.dot(
        rows, inverse_ref[1], preferred_element_type=F32
    )
    sum_ref[...] = total.reshape(2, RESIDUES, SUB, 2 * LANES)


def across_lags_kernel(offset, scale, mask_ref, cross_ref, twist_ref, inverse_ref, lag_ref, sum_ref):
    lag_sums(cross_ref, inverse_ref, sum_ref, True)
    weight = mask_ref[0, offset].astype(F32) * scale
    for group in range(2):
        for place, value in enumerate(lag_rows_of(sum_ref, group, twist_ref, weight)):
            for row in range(SUB):
                lag_ref[row % 4, group * 2 + row // 4, place * LANES : (place + 1) * LANES] = value[row]


def back_lags_kernel(
    scale, mask_ref, cross_ref, near_ref, across_ref, twist_ref, inverse_ref, out_ref, sum_ref, lag_ref, sem
):
    copies = [
        pltpu.make_async_copy(across_ref, out_ref.at[0], sem.at[0]),
        pltpu.make_async_copy(near_ref, out_ref.at[1], sem.at[1]),
    ]
    for copy in copies:
        copy.start()
    lag_sums(cross_ref, inverse_ref, sum_ref)
    weight = mask_ref[0, 2].astype(F32) * scale
    for group in range(2):
        for place, value in enumerate(lag_rows_of(sum_ref, group, twist_ref, weight)):
            for j in range(2):
                lag_ref[group * 2 + j, :, place * LANES : (place + 1) * LANES] = value[4 * j : 4 * j + 4]
        half = pl.ds(2 * group, 2)
        copies.append(pltpu.make_async_copy(lag_ref.at[half], out_ref.at[2, half], sem.at[2 + group]))
        copies[-1].start()
    for copy in copies:
        copy.wait()


def mirrored(records, filter_taps, segment_end, pair_mask, place, tables, scale):
    twist, dft, inverse, band = tables
    smem, vmem = pl.BlockSpec(memory_space=pltpu.SMEM), pl.BlockSpec(memory_space=VMEM)
    anywhere = pl.BlockSpec(memory_space=pl.ANY)
    blocks = lax.axis_size("chan")
    white = jax.ShapeDtypeStruct((2, 4, RESIDUES, SUB, LANES), BF16)
    spec = jax.ShapeDtypeStruct((2, RESIDUES, SUB, 2 * LANES), BF16)

    def exchange(array, axis):
        return lax.ppermute(array, axis, [(0, 1), (1, 0)])

    def along(array, by):
        return lax.ppermute(array, "chan", [(i, (i + by) % blocks) for i in range(blocks)])

    def across(array):
        pairs = [(0, 0), (1, 2), (2, 1), (3, 3)]
        return lax.ppermute(array, ("tm", "win"), pairs)

    keep, send = decimate(records, filter_taps, segment_end, place, 0)
    far_send, far_keep = along(send, 1), along(keep, 1)
    their_send, their_keep = exchange(send, "tm"), exchange(keep, "tm")
    relayed = exchange(far_send, "tm")
    own = pl.pallas_call(
        own_spectra_kernel,
        out_shape=jax.ShapeDtypeStruct((2, *white.shape), BF16),
        in_specs=[smem] + [vmem] * 7,
        out_specs=vmem,
        scratch_shapes=spectra_work(4),
        name="own_spectra",
        **params(COST[0]),
    )(place, keep, send, their_keep, their_send, twist, dft, band)
    own, relayed = lax.optimization_barrier((own, relayed))
    others = exchange(own, "win")
    far = pl.pallas_call(
        far_spectra_kernel,
        out_shape=white,
        in_specs=[smem] + [vmem] * 5,
        out_specs=vmem,
        scratch_shapes=spectra_work(4),
        name="far_spectra",
        **params(COST[1]),
    )(place, far_keep, relayed, twist, dft, band)
    fars = exchange(far, "win")
    cross = pl.pallas_call(
        far_cross_kernel,
        out_shape=spec,
        in_specs=[vmem] * 4,
        out_specs=vmem,
        name="far_cross",
        **params(COST[2]),
    )(own, others, far, fars)
    back, crossed = along(cross, -1), across(cross)
    lag = jax.ShapeDtypeStruct((4, 4, 2 * MAXLAG), F32)
    near = pl.pallas_call(
        functools.partial(near_pairs_kernel, 1, scale),
        out_shape=lag,
        in_specs=[smem, smem] + [vmem] * 4,
        out_specs=vmem,
        scratch_shapes=[VMEM((2, 2, 4, RESIDUES, SUB, LANES), BF16)] + lag_work(4, 4)[:3],
        name="near_pairs",
        **params(COST[3]),
    )(place, pair_mask, own, others, twist, inverse)
    side = pl.pallas_call(
        functools.partial(across_lags_kernel, 0, scale),
        out_shape=lag,
        in_specs=[smem] + [vmem] * 3,
        out_specs=vmem,
        scratch_shapes=lag_work(4, 4)[2:3],
        name="across_lags",
        **params(COST[4]),
    )(pair_mask, crossed, twist, inverse)
    return pl.pallas_call(
        functools.partial(back_lags_kernel, scale),
        out_shape=jax.ShapeDtypeStruct((3, 4, 4, 2 * MAXLAG), F32),
        in_specs=[smem] + [vmem] * 5,
        out_specs=anywhere,
        scratch_shapes=lag_work(4, 4)[2:4] + [pltpu.SemaphoreType.DMA((4,))],
        name="back_lags",
        **params(COST[4]),
    )(pair_mask, back, near, side, twist, inverse)


def spectra_work(groups):
    return [
        VMEM((groups, RESIDUES, SUB, 2 * LANES), BF16),
        VMEM((groups, RESIDUES, SUB, 2 * LANES), BF16),
        VMEM((groups, RESIDUES, SUB, 2 * LANES), F32),
        VMEM((groups, SUB, LANES), F32),
    ]


def lag_work(groups, owned):
    pair_groups = groups * owned // SUB
    return [
        VMEM((pair_groups, RESIDUES, SUB, 2 * LANES), BF16),
        VMEM((pair_groups, RESIDUES, SUB, 2 * LANES), BF16),
        VMEM((pair_groups, RESIDUES, SUB, 2 * LANES), F32),
        VMEM((groups, owned, 2 * MAXLAG), F32),
        pltpu.SemaphoreType.DMA,
    ]


def params(microseconds):
    return dict(
        compiler_params=pltpu.CompilerParams(vmem_limit_bytes=16 << 20),
        cost_estimate=pl.CostEstimate(
            flops=int(microseconds * 1e6), bytes_accessed=1 << 10, transcendentals=0
        ),
    )


def shards(records, filter_taps, segment_end, pair_mask):
    span = lax.axis_size("tm")
    owned = records.shape[0] // span
    groups = records.shape[0] // 2
    reach = (pair_mask.shape[1] - 1) // 2
    windows = 2 * records.shape[1]
    scale = 1.0 / math.sqrt(windows * ROWS * LANES // 2)
    place = jnp.stack([lax.axis_index("tm"), lax.axis_index("win")]).astype(jnp.int32)
    twist, dft, inverse, band = (
        jnp.asarray(t) for t in (twist_table(), forward_table(), inverse_table(), band_table())
    )
    smem, vmem = pl.BlockSpec(memory_space=pltpu.SMEM), pl.BlockSpec(memory_space=VMEM)
    anywhere = pl.BlockSpec(memory_space=pl.ANY)

    def permute(array, axis, by):
        count = lax.axis_size(axis)
        return lax.ppermute(array, axis, [(i, (i + by) % count) for i in range(count)])

    def segments(chunk):
        return [chunk] + [permute(chunk, "tm", -s) for s in range(1, span)]

    if span == 2 and reach == 1 and groups == 4:
        return mirrored(records, filter_taps, segment_end, pair_mask, place, (twist, dft, inverse, band), scale)
    keep, send = decimate(records, filter_taps, segment_end, place, 1)
    received = permute(send, "win", 1)
    block = join(keep, received)
    up = down = block
    moved = []
    for _ in range(reach):
        up, down = permute(up, "chan", 1), permute(down, "chan", -1)
        moved.append([up, down])
    mine = segments(block)
    white = pl.pallas_call(
        functools.partial(whiten_kernel, span),
        out_shape=(jax.ShapeDtypeStruct((2, groups, RESIDUES, SUB, LANES), BF16),) * 2,
        in_specs=[smem] + [vmem] * (span + 3),
        out_specs=(vmem,) * 2,
        scratch_shapes=spectra_work(groups),
        name="whiten",
        **params(3),
    )(place, *mine, twist, dft, band)
    other = [permute(part, "win", 1) for part in white]
    own, out = pl.pallas_call(
        functools.partial(own_pairs_kernel, owned, reach, scale),
        out_shape=(
            jax.ShapeDtypeStruct((2, 2, owned, RESIDUES, SUB, LANES), BF16),
            jax.ShapeDtypeStruct((2 * reach + 1, groups, owned, 2 * MAXLAG), F32),
        ),
        in_specs=[smem, smem] + [vmem] * 6,
        out_specs=(vmem, anywhere),
        scratch_shapes=lag_work(groups, owned),
        name="own_pairs",
        **params(2),
    )(place, pair_mask, *white, *other, twist, inverse)
    for step, sides in enumerate(moved):
        for side, far in zip((-1, 1), sides):
            offset = reach + side * (step + 1)
            out = pl.pallas_call(
                functools.partial(far_pairs_kernel, span, owned, offset, scale),
                out_shape=jax.ShapeDtypeStruct(out.shape, out.dtype),
                in_specs=[smem, smem] + [vmem] * (span + 5) + [anywhere],
                out_specs=anywhere,
                scratch_shapes=[VMEM((2, 2, groups, RESIDUES, SUB, LANES), BF16)]
                + spectra_work(groups)
                + lag_work(groups, owned),
                input_output_aliases={span + 7: 0},
                name="far_pairs",
                **params(4),
            )(place, pair_mask, *segments(far), own, twist, dft, band, inverse, out)
    return out


def solution(mesh):
    placed = (
        P(("fibre", "chan"), "win", "tm"),
        P(),
        P(("fibre", "win")),
        P(("fibre", "chan"), None),
    )
    return jax.shard_map(
        shards,
        mesh=mesh,
        in_specs=placed,
        out_specs=P(None, "win", ("fibre", "chan", "tm"), None),
        check_vma=False,
    )
```

```python
import functools
import math

import jax
import jax.numpy as jnp
import numpy as np
from jax import lax
from jax.experimental import pallas as pl
from jax.experimental.pallas import tpu as pltpu
from jax.sharding import PartitionSpec as P

MAXLAG = 1920
COST = (5000, 5000, 500, 500, 500)
BAND = 64
EPSILON = 1e-06

LANES = 128
ROWS = 32
RESIDUES = ROWS // 2 + 1
BLOCK = 4 * LANES
SUB = 8
F32 = jnp.float32
BF16 = jnp.bfloat16
VMEM = pltpu.VMEM


def halves(table):
    high = table.astype(np.float32).astype(jnp.bfloat16)
    low = (table - high.astype(np.float64)).astype(np.float32).astype(jnp.bfloat16)
    return np.stack([high, low])


def forward_table():
    angle = 2.0 * np.pi / LANES * (np.outer(np.arange(LANES), np.arange(LANES)) % LANES)
    cos, sin = np.cos(angle), np.sin(angle)
    return halves(np.block([[cos, -sin], [sin, cos]]))


def inverse_table():
    angle = 2.0 * np.pi / LANES * (np.outer(np.arange(LANES), np.arange(LANES)) % LANES)
    cos, sin = np.cos(angle), np.sin(angle)
    return halves(np.block([[cos, sin], [-sin, cos]]))


def twist_table():
    angle = 2.0 * np.pi / (ROWS * LANES) * np.outer(np.arange(RESIDUES), np.arange(LANES))
    both = np.stack([np.cos(angle), np.sin(angle)]).astype(np.float32)
    return np.ascontiguousarray(np.broadcast_to(both[:, :, None, :], (2, RESIDUES, SUB, LANES)))


def band_table():
    place = np.arange(LANES)
    place = np.minimum(place, LANES - 1 - place)
    band = place // (BAND // ROWS)
    return (band[:, None] == band[None, :]).astype(np.float32).astype(jnp.bfloat16)


def turn(value, k, n):
    real, imag = value
    c, s = math.cos(2 * math.pi * k / n), math.sin(2 * math.pi * k / n)
    if 8 * k == n:
        return ((real + imag) * c, (imag - real) * c)
    if 8 * k == 3 * n:
        return ((imag - real) * s, -(real + imag) * s)
    return (real * c + imag * s, imag * c - real * s)


def real_transform(x):
    n = len(x)
    if n == 2:
        return [(x[0] + x[1], None), (x[0] - x[1], None)]
    even, odd = real_transform(x[0::2]), real_transform(x[1::2])
    out = [None] * (n // 2 + 1)
    out[0] = (even[0][0] + odd[0][0], None)
    out[n // 2] = (even[0][0] - odd[0][0], None)
    for k in range(1, n // 4):
        er, ei = even[k]
        tr, ti = turn(odd[k], k, n)
        out[k] = (er + tr, ei + ti)
        out[n // 2 - k] = (er - tr, ti - ei)
    out[n // 4] = (even[n // 4][0], -odd[n // 4][0])
    return out


def real_inverse(x):
    n = 2 * (len(x) - 1)
    if n == 2:
        return [x[0][0] + x[1][0], x[0][0] - x[1][0]]
    even, odd = [None] * (n // 4 + 1), [None] * (n // 4 + 1)
    even[0] = (x[0][0] + x[n // 2][0], None)
    odd[0] = (x[0][0] - x[n // 2][0], None)
    for k in range(1, n // 4):
        ar, ai = x[k]
        br, bi = x[n // 2 - k]
        even[k] = (ar + br, ai - bi)
        dr, di = turn((ar - br, -(ai + bi)), k, n)
        odd[k] = (dr, -di)
    even[n // 4] = (2.0 * x[n // 4][0], None)
    odd[n // 4] = (-2.0 * x[n // 4][1], None)
    a, b = real_inverse(even), real_inverse(odd)
    return [v for pair in zip(a, b) for v in pair]


def split(value):
    high = value.astype(BF16)
    return high, (value - high.astype(F32)).astype(BF16)


def three_pass(high, low, table_ref):
    def dot(a, b):
        return jnp.dot(a, b, preferred_element_type=F32)

    return dot(high, table_ref[0]) + dot(low, table_ref[0]) + dot(high, table_ref[1])


def decimate_kernel(
    by, place_ref, end_hbm, taps_hbm, rec_hbm, keep_ref, send_ref,
    rec_ref, lhs_ref, taps_ref, end_ref, rec_sem, small_sem,
):
    channels, windows, length = rec_ref.shape
    half = channels // 2
    rows = half * windows
    blocks = length // BLOCK
    pieces = rec_sem.shape[0]
    piece = length // pieces
    taps = taps_hbm.shape[1]
    small = [
        pltpu.make_async_copy(end_hbm, end_ref, small_sem.at[0]),
        pltpu.make_async_copy(taps_hbm, taps_ref, small_sem.at[1]),
    ]
    copies = [
        pltpu.make_async_copy(
            rec_hbm.at[:, :, k * piece : (k + 1) * piece],
            rec_ref.at[:, :, k * piece : (k + 1) * piece],
            rec_sem.at[k],
        )
        for k in range(pieces)
    ]
    for copy in small + copies:
        copy.start()
    row = lax.broadcasted_iota(jnp.int32, (windows, BLOCK), 0)
    lane = lax.broadcasted_iota(jnp.int32, (windows, BLOCK), 1)
    tap = lax.broadcasted_iota(jnp.int32, (taps, BLOCK + LANES), 0)
    at = lax.broadcasted_iota(jnp.int32, (taps, BLOCK + LANES), 1)
    chosen = jnp.where(tap + at == LANES + 3, 1.0, 0.0).astype(BF16)
    for copy in small:
        copy.wait()
    base = jnp.dot(
        jnp.broadcast_to(taps_ref[...].astype(F32), (SUB, taps)).astype(BF16), chosen,
        preferred_element_type=F32,
    )
    tap_table = pltpu.roll(
        jnp.broadcast_to(base[0:1], (LANES, BLOCK + LANES)), 0, 1, stride=4, stride_axis=0
    ).astype(BF16)
    end = jnp.zeros((windows, BLOCK), jnp.int32)
    for w in range(windows):
        end = jnp.where(row == w, end_ref[w], end)
    end = end - place_ref[0] * length - lane
    for h in range(2):
        lhs_ref[h, 0, :, 0:LANES] = jnp.zeros((rows, LANES), BF16)
        lhs_ref[h, blocks, :, LANES:] = jnp.zeros((rows, BLOCK), BF16)
    for b in range(blocks):
        if b * BLOCK % piece == 0:
            copies[b * BLOCK // piece].wait()
        for h in range(2):
            side = place_ref[by] if h == 0 else 1 - place_ref[by]
            x = rec_ref[pl.ds(side * half, half), :, b * BLOCK : (b + 1) * BLOCK].astype(F32)
            x = jnp.where((end > b * BLOCK)[None], x, 0.0)
            x = x.reshape(rows, BLOCK).astype(BF16)
            lhs_ref[h, b, :, LANES:] = x
            lhs_ref[h, b + 1, :, 0:LANES] = x[:, BLOCK - LANES :]
    for h, out_ref in ((0, keep_ref), (1, send_ref)):
        out = lax.dot_general(
            lhs_ref[h].reshape((blocks + 1) * rows, BLOCK + LANES),
            tap_table,
            (((1,), (1,)), ((), ())),
            preferred_element_type=F32,
        )
        out_ref[...] = out.reshape(blocks + 1, half, windows, LANES).astype(BF16)


def decimate(records, filter_taps, segment_end, place, by):
    channels, windows, length = records.shape
    blocks = length // BLOCK
    piece = jax.ShapeDtypeStruct((blocks + 1, channels // 2, windows, LANES), BF16)
    return pl.pallas_call(
        functools.partial(decimate_kernel, by),
        out_shape=(piece, piece),
        in_specs=[pl.BlockSpec(memory_space=pltpu.SMEM)] + [pl.BlockSpec(memory_space=pltpu.HBM)] * 3,
        out_specs=(pl.BlockSpec(memory_space=VMEM),) * 2,
        scratch_shapes=[
            VMEM(records.shape, BF16),
            VMEM((2, blocks + 1, channels // 2 * windows, BLOCK + LANES), BF16),
            VMEM((1, filter_taps.shape[0]), BF16),
            pltpu.SMEM(segment_end.shape, jnp.int32),
            pltpu.SemaphoreType.DMA((4,)),
            pltpu.SemaphoreType.DMA((2,)),
        ],
        compiler_params=pltpu.CompilerParams(vmem_limit_bytes=24 << 20),
        cost_estimate=pl.CostEstimate(
            flops=2 * records.size // 4 * BLOCK, bytes_accessed=3 * records.size, transcendentals=0
        ),
        name="decimate",
    )(place, *(pltpu.with_memory_space_constraint(a, pltpu.HBM) for a in (segment_end, filter_taps.reshape(1, -1), records)))


def join_kernel(first_ref, second_ref, out_ref):
    out_ref[0] = first_ref[...]
    out_ref[1] = second_ref[...]


def join(first, second):
    vmem = pl.BlockSpec(memory_space=VMEM)
    return pl.pallas_call(
        join_kernel,
        out_shape=jax.ShapeDtypeStruct((2, *first.shape), first.dtype),
        in_specs=[vmem, vmem],
        out_specs=vmem,
        name="join",
        **params(0.2),
    )(first, second)


def spectra(load, flags, tables, work, store):
    twist_ref, dft_ref, band_ref = tables
    high_ref, low_ref, spec_ref, power_ref = work
    groups, span = high_ref.shape[0], len(flags)
    depth = ROWS // span

    def first(g, carry):
        x = []
        for s in range(span):
            for r in range(depth):
                value = load(s, r, g).astype(F32)
                if r == 0:
                    value = value + load((s - 1) % span, depth, g).astype(F32) * flags[s]
                x.append(value)
        for q, (real, imag) in enumerate(real_transform(x)):
            if q == 0:
                turned = (real, jnp.zeros_like(real))
            else:
                cos, sin = twist_ref[0, q], twist_ref[1, q]
                if imag is None:
                    turned = (real * cos, -(real * sin))
                else:
                    turned = (real * cos + imag * sin, imag * cos - real * sin)
            for part in range(2):
                high, low = split(turned[part])
                high_ref[g, q, :, part * LANES : (part + 1) * LANES] = high
                low_ref[g, q, :, part * LANES : (part + 1) * LANES] = low
        return carry

    for g in range(groups):
        first(g, 0)
    count = groups * RESIDUES * SUB
    spec = three_pass(
        high_ref[...].reshape(count, 2 * LANES), low_ref[...].reshape(count, 2 * LANES), dft_ref
    )
    spec_ref[...] = spec.reshape(groups, RESIDUES, SUB, 2 * LANES)
    lower = (lax.broadcasted_iota(jnp.int32, (SUB, LANES), 1) < LANES // 2).astype(F32)

    def powers(g, carry):
        ends = inner = None
        for q in range(RESIDUES):
            real, imag = spec_ref[g, q, :, :LANES], spec_ref[g, q, :, LANES:]
            power = real * real + imag * imag
            if q in (0, RESIDUES - 1):
                ends = power if ends is None else ends + power
            else:
                inner = power if inner is None else inner + power
        power_ref[g] = inner + ends * lower
        return carry

    for g in range(groups):
        powers(g, 0)
    high, low = split(power_ref[...].reshape(groups * SUB, LANES))
    energy = jnp.dot(high, band_ref[...], preferred_element_type=F32) + jnp.dot(
        low, band_ref[...], preferred_element_type=F32
    )
    power_ref[...] = lax.rsqrt(energy * (1.0 / BAND) + EPSILON).reshape(groups, SUB, LANES)
    lane = lax.broadcasted_iota(jnp.int32, (SUB, LANES), 1)
    nonzero = (lane > 0).astype(F32)

    def whiten(g, carry):
        scale = power_ref[g]
        for q in range(RESIDUES):
            factor = scale
            if q == 0:
                factor = scale * lower * nonzero
            elif q == RESIDUES - 1:
                factor = scale * lower
            for part in range(2):
                value = spec_ref[g, q, :, part * LANES : (part + 1) * LANES]
                store(part, g, q, (value * factor).astype(BF16))
        return carry

    for g in range(groups):
        whiten(g, 0)


def gather_rows(values):
    row = lax.broadcasted_iota(jnp.int32, (SUB, LANES), 0)
    step = SUB // 2
    while step:
        lower = (row % (2 * step)) < step
        values = [
            jnp.where(lower, a, b) + pltpu.roll(jnp.where(lower, b, a), step, 0)
            if step == SUB // 2
            else jnp.where(lower, a, b) + swap(jnp.where(lower, b, a), step, lower)
            for a, b in zip(values[:step], values[step:])
        ]
        step //= 2
    return values[0]


def swap(value, step, lower):
    return jnp.where(lower, pltpu.roll(value, SUB - step, 0), pltpu.roll(value, step, 0))


def cross_rows(owned, js, windows, part_of_own, part_of_remote):
    groups = []
    loaded = [[[part_of_own(w, p, i).astype(F32) for p in range(2)] for i in range(owned)] for w in range(windows)]
    for first in range(0, js * owned, SUB):
        real, imag = [], []
        for pair in range(first, first + SUB):
            j, i = pair // owned, pair % owned
            re = im = None
            for w in range(windows):
                ar, ai = loaded[w][i]
                br, bi = (part_of_remote(w, p, j).astype(F32) for p in range(2))
                r = ar * br + ai * bi
                m = ai * br - ar * bi
                re = r if re is None else re + r
                im = m if im is None else im + m
            real.append(re)
            imag.append(im)
        groups.append((gather_rows(real), gather_rows(imag)))
    return groups


def lag_rows_of(sum_ref, group, twist_ref, weight):
    x = []
    for q in range(RESIDUES):
        real, imag = sum_ref[group, q, :, :LANES], sum_ref[group, q, :, LANES:]
        if q == 0:
            x.append((real, None))
            continue
        cos, sin = twist_ref[0, q], twist_ref[1, q]
        turned = real * cos - imag * sin
        if q == RESIDUES - 1:
            x.append((turned, None))
        else:
            x.append((0.5 * turned, 0.5 * (real * sin + imag * cos)))
    out = real_inverse(x)
    count = MAXLAG // LANES
    return [out[a] * weight for a in (*range(ROWS - count, ROWS), *range(count))]


def correlate(own_load, remote_load, chunks, owned, remotes, tables, work, weight, lag_ref):
    twist_ref, inverse_ref = tables
    high_ref, low_ref, sum_ref = work
    pair_groups = remotes * owned // SUB
    for q in range(RESIDUES):
        rows = cross_rows(
            owned, remotes, chunks,
            lambda w, p, i: own_load(w, p, i, q), lambda w, p, j: remote_load(w, p, j, q),
        )
        for group, parts in enumerate(rows):
            for part, value in enumerate(parts):
                at = slice(part * LANES, (part + 1) * LANES)
                if low_ref is None:
                    high_ref[group, q, :, at] = value.astype(BF16)
                else:
                    high_ref[group, q, :, at], low_ref[group, q, :, at] = split(value)
    count = pair_groups * RESIDUES * SUB
    rows = high_ref[...].reshape(count, 2 * LANES)
    if low_ref is None:
        total = jnp.dot(rows, inverse_ref[0], preferred_element_type=F32) + jnp.dot(
            rows, inverse_ref[1], preferred_element_type=F32
        )
    else:
        total = three_pass(rows, low_ref[...].reshape(count, 2 * LANES), inverse_ref)
    sum_ref[...] = total.reshape(pair_groups, RESIDUES, SUB, 2 * LANES)
    per = SUB // owned
    for group in range(pair_groups):
        for place, value in enumerate(lag_rows_of(sum_ref, group, twist_ref, weight)):
            for j in range(per):
                lag_ref[group * per + j, :, place * LANES : (place + 1) * LANES] = value[
                    j * owned : (j + 1) * owned
                ]


def write_out(lag_ref, out_ref, offset, sem):
    copy = pltpu.make_async_copy(lag_ref, out_ref.at[offset], sem)
    copy.start()
    copy.wait()


def flags_of(place_ref, span):
    t = place_ref[0]
    return [((t + s) % span != 0).astype(F32) for s in range(span)]


def whiten_kernel(span, place_ref, *refs):
    pieces = refs[:span]
    twist_ref, dft_ref, band_ref = refs[span : span + 3]
    white_refs = refs[span + 3 : span + 5]
    work = refs[span + 5 :]
    flags = flags_of(place_ref, span)
    for c in range(2):

        def store(part, g, q, value, c=c):
            white_refs[c][part, g, q] = value

        def load(s, r, g, c=c):
            return pieces[s][c, r, g]

        spectra(load, flags, (twist_ref, dft_ref, band_ref), work, store)


def own_pairs_kernel(
    owned, offset, scale, place_ref, mask_ref, *refs,
):
    white_refs, other_refs = refs[:2], refs[2:4]
    twist_ref, inverse_ref, own_ref, out_ref, high_ref, low_ref, sum_ref, lag_ref, sem = refs[4:]
    groups = white_refs[0].shape[1]
    first = place_ref[0] * owned
    inside = lax.rem(first, groups)
    here = lax.div(first, groups) == place_ref[1]

    @pl.when(here)
    def _():
        for c in range(2):
            own_ref[c] = white_refs[c][:, pl.ds(inside, owned)]

    @pl.when(jnp.logical_not(here))
    def _():
        for c in range(2):
            own_ref[c] = other_refs[1 - c][:, pl.ds(inside, owned)]

    correlate(
        lambda c, p, i, q: own_ref[c, p, i, q],
        lambda c, p, j, q: white_refs[c][p, j, q],
        2, owned, groups, (twist_ref, inverse_ref), (high_ref, low_ref, sum_ref),
        mask_ref[0, offset].astype(F32) * scale, lag_ref,
    )
    write_out(lag_ref, out_ref, offset, sem)


def far_pairs_kernel(span, owned, offset, scale, place_ref, mask_ref, *refs):
    pieces = refs[:span]
    own_ref, twist_ref, dft_ref, band_ref, inverse_ref, _, out_ref = refs[span : span + 7]
    (
        white_ref, zhigh_ref, zlow_ref, spec_ref, power_ref, high_ref, low_ref, sum_ref, lag_ref, sem,
    ) = refs[span + 7 :]
    flags = flags_of(place_ref, span)
    groups = white_ref.shape[2]
    for c in range(2):

        def store(part, g, q, value, c=c):
            white_ref[c, part, g, q] = value

        def load(s, r, g, c=c):
            return pieces[s][c, r, g]

        spectra(
            load, flags, (twist_ref, dft_ref, band_ref),
            (zhigh_ref, zlow_ref, spec_ref, power_ref), store,
        )
    correlate(
        lambda c, p, i, q: own_ref[c, p, i, q],
        lambda c, p, j, q: white_ref[c, p, j, q],
        2, owned, groups, (twist_ref, inverse_ref), (high_ref, low_ref, sum_ref),
        mask_ref[0, offset].astype(F32) * scale, lag_ref,
    )
    write_out(lag_ref, out_ref, offset, sem)


def own_spectra_kernel(
    place_ref, keep_ref, send_ref, their_keep_ref, their_send_ref, twist_ref, dft_ref, band_ref, white_ref, *work
):
    flags = flags_of(place_ref, 2)
    for at, side in enumerate((1 - place_ref[1], place_ref[1])):
        kept = side == place_ref[0]

        def load(s, r, g, kept=kept):
            if s == 0:
                return jnp.where(kept, keep_ref[r, g], send_ref[r, g])
            return jnp.where(kept, their_send_ref[r, g], their_keep_ref[r, g])

        def store(part, g, q, value, at=at):
            white_ref[at, part, g, q] = value

        spectra(load, flags, (twist_ref, dft_ref, band_ref), work, store)


def far_spectra_kernel(place_ref, mine_ref, relayed_ref, twist_ref, dft_ref, band_ref, white_ref, *work):
    def load(s, r, g):
        return (mine_ref, relayed_ref)[s][r, g]

    def store(part, g, q, value):
        white_ref[part, g, q] = value

    spectra(load, flags_of(place_ref, 2), (twist_ref, dft_ref, band_ref), work, store)


def far_cross_kernel(white_ref, others_ref, far_ref, fars_ref, back_ref):
    own, far = (white_ref.at[1], others_ref.at[0]), (far_ref, fars_ref)
    for q in range(RESIDUES):
        rows = cross_rows(4, 4, 2, lambda w, p, j: far[w][p, j, q], lambda w, p, i: own[w][p, i, q])
        for group, parts in enumerate(rows):
            for part, value in enumerate(parts):
                at = slice(part * LANES, (part + 1) * LANES)
                back_ref[group, q, :, at] = value.astype(BF16)


def near_pairs_kernel(
    offset, scale, place_ref, mask_ref, white_ref, others_ref,
    twist_ref, inverse_ref, lag_ref, own_ref, high_ref, sum_ref,
):
    same = place_ref[0] == place_ref[1]

    @pl.when(same)
    def _():
        own_ref[0] = white_ref[1]
        own_ref[1] = others_ref[0]

    @pl.when(jnp.logical_not(same))
    def _():
        own_ref[0] = white_ref[0]
        own_ref[1] = others_ref[1]

    half = (white_ref.at[1], others_ref.at[0])
    correlate(
        lambda w, p, i, q: own_ref[w, p, i, q],
        lambda w, p, j, q: half[w][p, j, q],
        2, 4, 4, (twist_ref, inverse_ref), (high_ref, None, sum_ref),
        mask_ref[0, offset].astype(F32) * scale, lag_ref,
    )


def lag_sums(cross_ref, inverse_ref, sum_ref, conjugate=False):
    rows = cross_ref[...].reshape(2 * RESIDUES * SUB, 2 * LANES)
    if conjugate:
        rows = jnp.concatenate([rows[:, :LANES], -rows[:, LANES:]], axis=1)
    total = jnp.dot(rows, inverse_ref[0], preferred_element_type=F32) + jnp.dot(
        rows, inverse_ref[1], preferred_element_type=F32
    )
    sum_ref[...] = total.reshape(2, RESIDUES, SUB, 2 * LANES)


def across_lags_kernel(offset, scale, mask_ref, cross_ref, twist_ref, inverse_ref, lag_ref, sum_ref):
    lag_sums(cross_ref, inverse_ref, sum_ref, True)
    weight = mask_ref[0, offset].astype(F32) * scale
    for group in range(2):
        for place, value in enumerate(lag_rows_of(sum_ref, group, twist_ref, weight)):
            for row in range(SUB):
                lag_ref[row % 4, group * 2 + row // 4, place * LANES : (place + 1) * LANES] = value[row]


def back_lags_kernel(
    scale, mask_ref, cross_ref, near_ref, across_ref, twist_ref, inverse_ref, out_ref, sum_ref, lag_ref, sem
):
    copies = [
        pltpu.make_async_copy(across_ref, out_ref.at[0], sem.at[0]),
        pltpu.make_async_copy(near_ref, out_ref.at[1], sem.at[1]),
    ]
    for copy in copies:
        copy.start()
    lag_sums(cross_ref, inverse_ref, sum_ref)
    weight = mask_ref[0, 2].astype(F32) * scale
    for group in range(2):
        for place, value in enumerate(lag_rows_of(sum_ref, group, twist_ref, weight)):
            for j in range(2):
                lag_ref[group * 2 + j, :, place * LANES : (place + 1) * LANES] = value[4 * j : 4 * j + 4]
        half = pl.ds(2 * group, 2)
        copies.append(pltpu.make_async_copy(lag_ref.at[half], out_ref.at[2, half], sem.at[2 + group]))
        copies[-1].start()
    for copy in copies:
        copy.wait()


def mirrored(records, filter_taps, segment_end, pair_mask, place, tables, scale):
    twist, dft, inverse, band = tables
    smem, vmem = pl.BlockSpec(memory_space=pltpu.SMEM), pl.BlockSpec(memory_space=VMEM)
    anywhere = pl.BlockSpec(memory_space=pl.ANY)
    blocks = lax.axis_size("chan")
    white = jax.ShapeDtypeStruct((2, 4, RESIDUES, SUB, LANES), BF16)
    spec = jax.ShapeDtypeStruct((2, RESIDUES, SUB, 2 * LANES), BF16)

    def exchange(array, axis):
        return lax.ppermute(array, axis, [(0, 1), (1, 0)])

    def along(array, by):
        return lax.ppermute(array, "chan", [(i, (i + by) % blocks) for i in range(blocks)])

    def across(array):
        pairs = [(0, 0), (1, 2), (2, 1), (3, 3)]
        return lax.ppermute(array, ("tm", "win"), pairs)

    keep, send = decimate(records, filter_taps, segment_end, place, 0)
    far_send, far_keep = along(send, 1), along(keep, 1)
    their_send, their_keep = exchange(send, "tm"), exchange(keep, "tm")
    relayed = exchange(far_send, "tm")
    own = pl.pallas_call(
        own_spectra_kernel,
        out_shape=jax.ShapeDtypeStruct((2, *white.shape), BF16),
        in_specs=[smem] + [vmem] * 7,
        out_specs=vmem,
        scratch_shapes=spectra_work(4),
        name="own_spectra",
        **params(COST[0]),
    )(place, keep, send, their_keep, their_send, twist, dft, band)
    own, relayed = lax.optimization_barrier((own, relayed))
    others = exchange(own, "win")
    far = pl.pallas_call(
        far_spectra_kernel,
        out_shape=white,
        in_specs=[smem] + [vmem] * 5,
        out_specs=vmem,
        scratch_shapes=spectra_work(4),
        name="far_spectra",
        **params(COST[1]),
    )(place, far_keep, relayed, twist, dft, band)
    fars = exchange(far, "win")
    cross = pl.pallas_call(
        far_cross_kernel,
        out_shape=spec,
        in_specs=[vmem] * 4,
        out_specs=vmem,
        name="far_cross",
        **params(COST[2]),
    )(own, others, far, fars)
    back, crossed = along(cross, -1), across(cross)
    lag = jax.ShapeDtypeStruct((4, 4, 2 * MAXLAG), F32)
    near = pl.pallas_call(
        functools.partial(near_pairs_kernel, 1, scale),
        out_shape=lag,
        in_specs=[smem, smem] + [vmem] * 4,
        out_specs=vmem,
        scratch_shapes=[VMEM((2, 2, 4, RESIDUES, SUB, LANES), BF16)] + lag_work(4, 4)[1:3],
        name="near_pairs",
        **params(COST[3]),
    )(place, pair_mask, own, others, twist, inverse)
    side = pl.pallas_call(
        functools.partial(across_lags_kernel, 0, scale),
        out_shape=lag,
        in_specs=[smem] + [vmem] * 3,
        out_specs=vmem,
        scratch_shapes=lag_work(4, 4)[2:3],
        name="across_lags",
        **params(COST[4]),
    )(pair_mask, crossed, twist, inverse)
    return pl.pallas_call(
        functools.partial(back_lags_kernel, scale),
        out_shape=jax.ShapeDtypeStruct((3, 4, 4, 2 * MAXLAG), F32),
        in_specs=[smem] + [vmem] * 5,
        out_specs=anywhere,
        scratch_shapes=lag_work(4, 4)[2:4] + [pltpu.SemaphoreType.DMA((4,))],
        name="back_lags",
        **params(COST[4]),
    )(pair_mask, back, near, side, twist, inverse)


def spectra_work(groups):
    return [
        VMEM((groups, RESIDUES, SUB, 2 * LANES), BF16),
        VMEM((groups, RESIDUES, SUB, 2 * LANES), BF16),
        VMEM((groups, RESIDUES, SUB, 2 * LANES), F32),
        VMEM((groups, SUB, LANES), F32),
    ]


def lag_work(groups, owned):
    pair_groups = groups * owned // SUB
    return [
        VMEM((pair_groups, RESIDUES, SUB, 2 * LANES), BF16),
        VMEM((pair_groups, RESIDUES, SUB, 2 * LANES), BF16),
        VMEM((pair_groups, RESIDUES, SUB, 2 * LANES), F32),
        VMEM((groups, owned, 2 * MAXLAG), F32),
        pltpu.SemaphoreType.DMA,
    ]


def params(microseconds):
    return dict(
        compiler_params=pltpu.CompilerParams(vmem_limit_bytes=16 << 20),
        cost_estimate=pl.CostEstimate(
            flops=int(microseconds * 1e6), bytes_accessed=1 << 10, transcendentals=0
        ),
    )


def shards(records, filter_taps, segment_end, pair_mask):
    span = lax.axis_size("tm")
    owned = records.shape[0] // span
    groups = records.shape[0] // 2
    reach = (pair_mask.shape[1] - 1) // 2
    windows = 2 * records.shape[1]
    scale = 1.0 / math.sqrt(windows * ROWS * LANES // 2)
    place = jnp.stack([lax.axis_index("tm"), lax.axis_index("win")]).astype(jnp.int32)
    twist, dft, inverse, band = (
        jnp.asarray(t) for t in (twist_table(), forward_table(), inverse_table(), band_table())
    )
    smem, vmem = pl.BlockSpec(memory_space=pltpu.SMEM), pl.BlockSpec(memory_space=VMEM)
    anywhere = pl.BlockSpec(memory_space=pl.ANY)

    def permute(array, axis, by):
        count = lax.axis_size(axis)
        return lax.ppermute(array, axis, [(i, (i + by) % count) for i in range(count)])

    def segments(chunk):
        return [chunk] + [permute(chunk, "tm", -s) for s in range(1, span)]

    if span == 2 and reach == 1 and groups == 4:
        return mirrored(records, filter_taps, segment_end, pair_mask, place, (twist, dft, inverse, band), scale)
    keep, send = decimate(records, filter_taps, segment_end, place, 1)
    received = permute(send, "win", 1)
    block = join(keep, received)
    up = down = block
    moved = []
    for _ in range(reach):
        up, down = permute(up, "chan", 1), permute(down, "chan", -1)
        moved.append([up, down])
    mine = segments(block)
    white = pl.pallas_call(
        functools.partial(whiten_kernel, span),
        out_shape=(jax.ShapeDtypeStruct((2, groups, RESIDUES, SUB, LANES), BF16),) * 2,
        in_specs=[smem] + [vmem] * (span + 3),
        out_specs=(vmem,) * 2,
        scratch_shapes=spectra_work(groups),
        name="whiten",
        **params(3),
    )(place, *mine, twist, dft, band)
    other = [permute(part, "win", 1) for part in white]
    own, out = pl.pallas_call(
        functools.partial(own_pairs_kernel, owned, reach, scale),
        out_shape=(
            jax.ShapeDtypeStruct((2, 2, owned, RESIDUES, SUB, LANES), BF16),
            jax.ShapeDtypeStruct((2 * reach + 1, groups, owned, 2 * MAXLAG), F32),
        ),
        in_specs=[smem, smem] + [vmem] * 6,
        out_specs=(vmem, anywhere),
        scratch_shapes=lag_work(groups, owned),
        name="own_pairs",
        **params(2),
    )(place, pair_mask, *white, *other, twist, inverse)
    for step, sides in enumerate(moved):
        for side, far in zip((-1, 1), sides):
            offset = reach + side * (step + 1)
            out = pl.pallas_call(
                functools.partial(far_pairs_kernel, span, owned, offset, scale),
                out_shape=jax.ShapeDtypeStruct(out.shape, out.dtype),
                in_specs=[smem, smem] + [vmem] * (span + 5) + [anywhere],
                out_specs=anywhere,
                scratch_shapes=[VMEM((2, 2, groups, RESIDUES, SUB, LANES), BF16)]
                + spectra_work(groups)
                + lag_work(groups, owned),
                input_output_aliases={span + 7: 0},
                name="far_pairs",
                **params(4),
            )(place, pair_mask, *segments(far), own, twist, dft, band, inverse, out)
    return out


def solution(mesh):
    placed = (
        P(("fibre", "chan"), "win", "tm"),
        P(),
        P(("fibre", "win")),
        P(("fibre", "chan"), None),
    )
    return jax.shard_map(
        shards,
        mesh=mesh,
        in_specs=placed,
        out_specs=P(None, "win", ("fibre", "chan", "tm"), None),
        check_vma=False,
    )
```
